32 devices in a mesh: curve: 8 (over y, x, core), sub: 4 (over z).
Axes of the slice: x: 2, y: 2, z: 4, core: 2. Of those that a mesh axis runs over, the one named last changes fastest.
Arguments:
- populations: float32 [19, 2048, 256], P(None, ('curve', 'sub')), may hold values from 0.2 to 1.8
- count_old: int32 [8, 4], replicated, may hold values from 2 to 4, as said below
- count_new: int32 [8, 4], replicated, may hold values from 2 to 4, as said below
Outputs:
- evolved: float32 [19, 2048, 256], P(None, ('curve', 'sub'))
The draws below stay inside these ranges and needn't reach their ends.
Inputs may be any that keep to these rules, and one draw needn't show every extreme that they name: Each row of count_old sums to 3 times the number of devices along sub, so the blocks of a curve segment stay within it; every row has an entry 4. Each row of count_new sums to 3 times the number of devices along sub and has an entry 4. Between count_old and count_new each boundary between the runs of two neighbouring devices moves by at most one block, and in every row one boundary moves, so every block's new owner is its old owner or the device beside it on sub.
All inputs are finite; a program needn't handle non-finite values.
Results may differ from the reference program's by a relative error of at most 0.00002.
Values sent between devices are 32-bit elements; how exact they have to be, the bound alone decides.
No kernel may reach another device: no remote copies, remote signals or barrier semaphores. Data moves between devices by JAX's collectives and lax.ppermute only.
A program may use at most 64 MiB of HBM per device.

```python
import jax
import jax.numpy as jnp
import numpy as np
from jax import lax

BX = 16
BY = 16
BZ = 16
AVG = 3
STEPS = 4
SLOTS = 4
PLANES = 2048
CROSS = 256
N_CURVE = 8
N_SUB = 4


def chain_counts(key):
    base = jax.random.fold_in(key, 31)
    bits_old = jax.random.randint(jax.random.fold_in(base, 1), (N_CURVE, N_SUB), 0, 2)
    bits_new = jax.random.randint(jax.random.fold_in(base, 2), (N_CURVE, N_SUB), 0, 2)
    chosen = jax.random.randint(jax.random.fold_in(base, 3), (N_CURVE, 1), 0, N_SUB - 1)
    second = (chosen + 1) % (N_SUB - 1)
    column = jnp.arange(N_SUB, dtype=jnp.int32)[None, :]
    bits_old = jnp.where(column == chosen, 1, bits_old)
    bits_old = jnp.where(column == chosen - 1, 0, bits_old)
    bits_new = jnp.where(column == chosen, 0, bits_new)
    bits_new = jnp.where(column == second, 1, bits_new)
    bits_new = jnp.where(column == second - 1, 0, bits_new)
    bits_old = jnp.where(column == N_SUB - 1, 0, bits_old)
    bits_new = jnp.where(column == N_SUB - 1, 0, bits_new)
    leading = jnp.zeros((N_CURVE, 1), jnp.int32)
    before_old = jnp.concatenate([leading, bits_old[:, :-1]], axis=1)
    before_new = jnp.concatenate([leading, bits_new[:, :-1]], axis=1)
    counts_old = (AVG + bits_old - before_old).astype(jnp.int32)
    counts_new = (AVG + bits_new - before_new).astype(jnp.int32)
    return (counts_old, counts_new)


def draw_count_old(key, part):
    return chain_counts(key)[0]


def draw_count_new(key, part):
    return chain_counts(key)[1]


def block_scale(key, dims, shards, low, largest):
    gain, own = 1.0, jax.random.fold_in(key, 6)
    for axis_at, shards_of in shards:
        heights = jnp.exp(jax.random.uniform(jax.random.fold_in(own, axis_at), (shards_of,), jnp.float32, low / len(shards), largest / len(shards)))
        gain = gain * jnp.repeat(heights, dims[axis_at] // shards_of).reshape([-1 if axis == axis_at else 1 for axis in range(len(dims))])
    return gain


def setup_inputs(seed: int = 0) -> dict:
    splits = jax.random.split(jax.random.key(seed), 4)
    return {
        "populations": jnp.clip(0.2 + 1.5999999 * jax.random.uniform(splits[0], (19, PLANES, CROSS), jnp.float32) ** block_scale(splits[0], (19, PLANES, CROSS), ((1, 32),), -0.2, 0.2), 0.2, 1.8),
        "count_old": draw_count_old(jax.random.fold_in(splits[3], 71), 0),
        "count_new": draw_count_new(jax.random.fold_in(splits[3], 71), 0),
    }


VELOCITY = np.array([[0, 0, 0], [1, 0, 0], [1, 1, 0], [1, -1, 0], [1, 0, 1], [1, 0, -1], [-1, 0, 0], [-1, 1, 0], [-1, -1, 0], [-1, 0, 1], [-1, 0, -1], [0, 1, 0], [0, -1, 0], [0, 0, 1], [0, 0, -1], [0, 1, 1], [0, 1, -1], [0, -1, 1], [0, -1, -1]])
WEIGHTS = np.array([1.0 / 3.0] + [1.0 / 18.0, 1.0 / 36.0, 1.0 / 36.0, 1.0 / 36.0, 1.0 / 36.0] * 2 + [1.0 / 18.0] * 4 + [1.0 / 36.0] * 4)
tau_base = 0.6
smagorinsky = 0.17

def collide(lattice):
    weighted = [float(WEIGHTS[direction]) * lattice[direction] for direction in range(19)]
    density = weighted[0]
    for direction in range(1, 19):
        density = density + weighted[direction]
    velocity = []
    for component in range(3):
        moment = jnp.zeros_like(density)
        for direction in range(19):
            factor = int(VELOCITY[direction, component])
            if factor != 0:
                moment = moment + factor * weighted[direction]
        velocity.append(moment / density)
    speed_square = velocity[0] * velocity[0] + velocity[1] * velocity[1] + velocity[2] * velocity[2]
    departure = []
    for direction in range(19):
        along = jnp.zeros_like(density)
        for component in range(3):
            factor = int(VELOCITY[direction, component])
            if factor != 0:
                along = along + factor * velocity[component]
        balance = density * (1.0 + 3.0 * along + 4.5 * along * along - 1.5 * speed_square)
        departure.append(lattice[direction] - balance)
    pairs = [(0, 0), (1, 1), (2, 2), (0, 1), (0, 2), (1, 2)]
    stress = []
    for first_axis, second_axis in pairs:
        total = jnp.zeros_like(density)
        for direction in range(19):
            factor = int(VELOCITY[direction, first_axis]) * int(VELOCITY[direction, second_axis])
            if factor != 0:
                total = total + factor * float(WEIGHTS[direction]) * departure[direction]
        stress.append(total)
    magnitude = jnp.sqrt(stress[0] * stress[0] + stress[1] * stress[1] + stress[2] * stress[2] + 2.0 * (stress[3] * stress[3] + stress[4] * stress[4] + stress[5] * stress[5]))
    relax_time = 0.5 * (tau_base + jnp.sqrt(tau_base * tau_base + 18.0 * np.sqrt(2.0) * smagorinsky * smagorinsky * magnitude / density))
    return jnp.stack([lattice[direction] - departure[direction] / relax_time for direction in range(19)])

def propagate(relaxed):
    cube = relaxed.reshape(19, relaxed.shape[1], BY, BZ)
    moved = [jnp.roll(cube[direction], (int(VELOCITY[direction, 0]), int(VELOCITY[direction, 1]), int(VELOCITY[direction, 2])), axis=(0, 1, 2)) for direction in range(19)]
    return jnp.stack(moved).reshape(relaxed.shape)

def reference(populations, count_old, count_new):
    group_blocks = AVG * N_SUB
    total_blocks = group_blocks * N_CURVE
    blocks = jnp.arange(total_blocks, dtype=jnp.int32)
    group = blocks // group_blocks
    within = blocks % group_blocks
    old_ends = jnp.cumsum(count_old, axis=1).astype(jnp.int32)
    old_starts = old_ends - count_old
    owner = lax.optimization_barrier(jnp.sum((old_ends[group] <= within[:, None]).astype(jnp.int32), axis=1)).astype(jnp.int32)
    owner = jnp.minimum(owner, N_SUB - 1)
    slot_index = within - old_starts[group, owner]
    source_block = (group * N_SUB + owner) * SLOTS + slot_index
    source_plane = (source_block[:, None] * BX + jnp.arange(BX, dtype=jnp.int32)[None, :]).reshape(-1)
    lattice = jnp.take(populations, source_plane, axis=1)
    for step_index in range(STEPS):
        lattice = propagate(collide(lattice))
    new_ends = jnp.cumsum(count_new, axis=1).astype(jnp.int32)
    new_starts = new_ends - count_new
    planes = jnp.arange(populations.shape[1], dtype=jnp.int32)
    device = planes // (SLOTS * BX)
    slot_new = planes // BX % SLOTS
    row_index = device // N_SUB
    column_index = device % N_SUB
    alive = slot_new < count_new[row_index, column_index]
    target_block = row_index * group_blocks + new_starts[row_index, column_index] + slot_new
    target_plane = jnp.clip(target_block * BX + planes % BX, 0, total_blocks * BX - 1).astype(jnp.int32)
    picked = jnp.take(lattice, target_plane, axis=1)
    return jnp.where(alive[None, :, None], picked, jnp.zeros_like(picked))
```

```python
import functools

import jax
import jax.numpy as jnp
import numpy as np
from jax import lax
from jax.experimental import pallas as pl
from jax.experimental.pallas import tpu as pltpu
from jax.sharding import PartitionSpec as P

BX = 16
BZ = 16
STEPS = 4
DIRS = 19
REACH = BX + STEPS
LANES = 128
HALVES = 2
HOME = 40
TOP = 8

VELOCITY = np.array(
    [
        [0, 0, 0],
        [1, 0, 0],
        [1, 1, 0],
        [1, -1, 0],
        [1, 0, 1],
        [1, 0, -1],
        [-1, 0, 0],
        [-1, 1, 0],
        [-1, -1, 0],
        [-1, 0, 1],
        [-1, 0, -1],
        [0, 1, 0],
        [0, -1, 0],
        [0, 0, 1],
        [0, 0, -1],
        [0, 1, 1],
        [0, 1, -1],
        [0, -1, 1],
        [0, -1, -1],
    ]
)
tau_base = 0.6
smagorinsky = 0.17


def collide(h):
    def pair(first, second):
        return h[first] + h[second], h[first] - h[second]

    s_x, d_x = pair(1, 6)
    s_xyp, d_xyp = pair(2, 8)
    s_xym, d_xym = pair(3, 7)
    s_xzp, d_xzp = pair(4, 10)
    s_xzm, d_xzm = pair(5, 9)
    s_y, d_y = pair(11, 12)
    s_z, d_z = pair(13, 14)
    s_yzp, d_yzp = pair(15, 18)
    s_yzm, d_yzm = pair(16, 17)
    j_x = (d_x + d_x) + (d_xyp + d_xym) + (d_xzp + d_xzm)
    j_y = (d_y + d_y) + (d_xyp - d_xym) + (d_yzp + d_yzm)
    j_z = (d_z + d_z) + (d_xzp - d_xzm) + (d_yzp - d_yzm)
    t_xy, t_xz, t_yz = s_xyp + s_xym, s_xzp + s_xzm, s_yzp + s_yzm
    m_xy, m_xz, m_yz = s_xyp - s_xym, s_xzp - s_xzm, s_yzp - s_yzm
    ss_x, ss_y, ss_z = s_x + s_x, s_y + s_y, s_z + s_z
    yz_part = ss_y + t_yz
    m_xx = ss_x + (t_xy + t_xz)
    m_yy = yz_part + t_xy
    m_zz = ss_z + (t_xz + t_yz)
    rho36 = (12.0 * h[0] + ss_z) + (m_xx + yz_part)
    inverse = 1.0 / rho36
    k_u = 1.5 * inverse
    k_p = 2.25 * inverse
    u_x, u_y, u_z = j_x * k_u, j_y * k_u, j_z * k_u
    xx, yy, zz = u_x * u_x, u_y * u_y, u_z * u_z
    xy, xz, yz = u_x * u_y, u_x * u_z, u_y * u_z
    p_xx = m_xx * k_p - (xx + 0.75)
    p_yy = m_yy * k_p - (yy + 0.75)
    p_zz = m_zz * k_p - (zz + 0.75)
    p_xy = m_xy * k_p - xy
    p_xz = m_xz * k_p - xz
    p_yz = m_yz * k_p - yz
    off = p_xy * p_xy + p_xz * p_xz + p_yz * p_yz
    square = (p_xx * p_xx + p_yy * p_yy) + (p_zz * p_zz + (off + off))
    magnitude = jnp.sqrt(square)
    factor = 18.0 * np.sqrt(2.0) * smagorinsky * smagorinsky / 2.25
    inner = tau_base * tau_base + float(factor) * magnitude
    omega = 2.0 / (tau_base + inner * lax.rsqrt(inner))
    keep = 1.0 - omega
    gain = (omega * (1.0 / 36.0)) * rho36
    gain2 = gain + gain
    rest = gain - gain * ((2.0 / 3.0) * ((xx + yy) + zz))
    gain4 = gain2 + gain2
    a_x, a_y, a_z = gain2 * u_x, gain2 * u_y, gain2 * u_z
    b_x, b_y, b_z = a_x * u_x, a_y * u_y, a_z * u_z
    n_x, n_y, n_z = rest + b_x, rest + b_y, rest + b_z
    out = [None] * DIRS
    out[0] = keep * h[0] + rest

    def spread(first, second, even, odd):
        out[first] = keep * h[first] + (even + odd)
        out[second] = keep * h[second] + (even - odd)

    spread(1, 6, n_x, a_x)
    spread(11, 12, n_y, a_y)
    spread(13, 14, n_z, a_z)
    for plus, minus, base, cross, first, second in (
        ((2, 8), (3, 7), n_x + b_y, gain4 * xy, a_x, a_y),
        ((4, 10), (5, 9), n_x + b_z, gain4 * xz, a_x, a_z),
        ((15, 18), (16, 17), n_y + b_z, gain4 * yz, a_y, a_z),
    ):
        spread(*plus, base + cross, first + second)
        spread(*minus, base - cross, first - second)
    return out


def lane_sources(step_y, step_z):
    lane = lax.broadcasted_iota(jnp.int32, (8, LANES), 1)
    along_y = (lane - step_y * BZ) & (LANES - 1) & ~(BZ - 1)
    along_z = (lane - step_z) & (BZ - 1)
    return along_y | along_z


def moves():
    lane = lax.broadcasted_iota(jnp.int32, (8, LANES), 1)
    index = {}
    for step_y in (-1, 0, 1):
        for step_z in (-1, 1):
            index[step_y, step_z] = lane_sources(step_y, step_z)
    border = {1: lane < BZ, -1: lane >= LANES - BZ}
    return index, border


def shift_cross(lower, upper, direction, tables):
    index, border = tables
    step_y, step_z = int(VELOCITY[direction, 1]), int(VELOCITY[direction, 2])
    if step_z != 0:
        source = index[step_y, step_z]
        lower = jnp.take_along_axis(lower, source, axis=1, mode="promise_in_bounds")
        upper = jnp.take_along_axis(upper, source, axis=1, mode="promise_in_bounds")
    elif step_y != 0:
        lower = pltpu.roll(lower, (step_y * BZ) % LANES, 1)
        upper = pltpu.roll(upper, (step_y * BZ) % LANES, 1)
    if step_y != 0:
        edge = border[step_y]
        lower, upper = jnp.where(edge, upper, lower), jnp.where(edge, lower, upper)
    return lower, upper


def layout_of(sub_count, old_ref, new_ref, curve, sub):
    old_start, new_start = 0, 0
    for other in range(sub_count - 1):
        before = other < sub
        old_start += jnp.where(before, old_ref[other, curve], 0)
        new_start += jnp.where(before, new_ref[other, curve], 0)
    held_old = old_ref[sub, curve] * BX
    held_new = new_ref[sub, curve] * BX
    return held_old, held_new, (new_start - old_start) * BX


def pack_kernel(sub_count, old_ref, new_ref, pop_ref, one_ref, two_ref, far_ref, all_ref, sem):
    curve, sub = lax.axis_index("curve"), lax.axis_index("sub")
    loads = [
        pltpu.make_async_copy(pop_ref.at[:, :, half * LANES : (half + 1) * LANES], all_ref.at[:, half], sem.at[half])
        for half in range(HALVES)
    ]
    for load in loads:
        load.start()
    held_old, _, _ = layout_of(sub_count, old_ref, new_ref, curve, sub)
    for load in loads:
        load.wait()
    even = sub % 2 == 0
    right = held_old - REACH
    one_start = jnp.where(even, right, 0)
    two_start = jnp.where(even, 0, right)
    far_start = jnp.where(sub == 0, 0, held_old - STEPS)
    for target, start, count in (
        (one_ref, one_start, REACH),
        (two_ref, two_start, REACH),
        (far_ref, far_start, STEPS),
    ):
        for direction in range(DIRS):
            for half in range(HALVES):
                row = (direction * HALVES + half) * count
                target[row : row + count, :] = all_ref[direction, half, pl.ds(start, count), :]


def step_kernel(
    sub_count, slots, old_ref, new_ref, pop_ref, one_ref, two_ref, far_ref, out_ref,
    first_ref, ping_ref, pong_ref, sem,
):
    curve, sub = lax.axis_index("curve"), lax.axis_index("sub")
    held_old, held_new, offset = layout_of(sub_count, old_ref, new_ref, curve, sub)
    home = pl.multiple_of(HOME - offset, 8)
    loads = [
        pltpu.make_async_copy(
            pop_ref.at[:, :, half * LANES : (half + 1) * LANES],
            first_ref.at[:, half, pl.ds(home, slots * BX), :],
            sem.at[half],
        )
        for half in range(HALVES)
    ]
    for load in loads:
        load.start()
    for load in loads:
        load.wait()

    def place(source, count, start):
        for direction in range(DIRS):
            for half in range(HALVES):
                row = (direction * HALVES + half) * count
                first_ref[direction, half, pl.ds(start, count), :] = source[row : row + count, :]

    even = sub % 2 == 0
    left_row, right_row = home - REACH, home + held_old

    @pl.when(even)
    def _():
        place(one_ref, REACH, right_row)

    @pl.when(jnp.logical_not(even))
    def _():
        place(one_ref, REACH, left_row)

    @pl.when(jnp.logical_and(even, sub > 0))
    def _():
        place(two_ref, REACH, left_row)

    @pl.when(jnp.logical_and(jnp.logical_not(even), sub < sub_count - 1))
    def _():
        place(two_ref, REACH, right_row)

    @pl.when(sub == 0)
    def _():
        place(far_ref, STEPS, home - STEPS)

    @pl.when(sub == sub_count - 1)
    def _():
        place(far_ref, STEPS, right_row)

    tables = moves()
    groups = held_new // 8 + 1

    def run(source, target, base, moving):
        def body(group, carry):
            row = base + group * 8
            relaxed = []
            for half in range(HALVES):
                cells = []
                for direction in range(DIRS):
                    at = row - int(VELOCITY[direction, 0]) if moving else row
                    cells.append(source[direction, half, pl.ds(at, 8), :])
                relaxed.append(collide(cells))
            to = pl.multiple_of(TOP + group * 8, 8)
            for direction in range(DIRS):
                lower, upper = shift_cross(relaxed[0][direction], relaxed[1][direction], direction, tables)
                target[direction, 0, pl.ds(to, 8), :] = lower
                target[direction, 1, pl.ds(to, 8), :] = upper
            return carry

        lax.fori_loop(0, groups, body, 0)

    run(first_ref, ping_ref, HOME - STEPS, False)
    run(ping_ref, pong_ref, TOP + 1, True)
    run(pong_ref, ping_ref, TOP + 1, True)
    run(ping_ref, pong_ref, TOP + 1, True)
    live = held_new // 8
    for group in range(slots * BX // 8):

        @pl.when(group < live)
        def _():
            for direction in range(DIRS):
                row = TOP + 1 + group * 8 - int(VELOCITY[direction, 0])
                for half in range(HALVES):
                    out_ref[direction, group * 8 : group * 8 + 8, half * LANES : (half + 1) * LANES] = pong_ref[
                        direction, half, row : row + 8, :
                    ]

        @pl.when(group >= live)
        def _():
            for direction in range(DIRS):
                out_ref[direction, group * 8 : group * 8 + 8, :] = jnp.zeros((8, HALVES * LANES), jnp.float32)


def shards(populations, count_old, count_new):
    curve_count, sub_count = lax.axis_size("curve"), lax.axis_size("sub")
    planes = populations.shape[1]
    slots = planes // BX
    total = curve_count * sub_count
    old, new = count_old.T, count_new.T
    smem = pl.BlockSpec(memory_space=pltpu.SMEM)
    hbm = pl.BlockSpec(memory_space=pl.ANY)
    vmem = pl.BlockSpec(memory_space=pltpu.VMEM)
    rows = DIRS * HALVES
    near = jax.ShapeDtypeStruct((rows * REACH, LANES), jnp.float32)
    far = jax.ShapeDtypeStruct((rows * STEPS, LANES), jnp.float32)
    one, two, rim = pl.pallas_call(
        functools.partial(pack_kernel, sub_count),
        out_shape=(near, near, far),
        in_specs=[smem, smem, hbm],
        out_specs=(vmem, vmem, vmem),
        scratch_shapes=[
            pltpu.VMEM((DIRS, HALVES, planes, LANES), jnp.float32),
            pltpu.SemaphoreType.DMA((HALVES,)),
        ],
        name="pack",
    )(old, new, populations)
    both = ("curve", "sub")
    inside = [(at, at ^ 1) for at in range(total)]
    between, across = [], []
    for at in range(1, total, 2):
        after = (at + 1) % total
        into = across if after % sub_count == 0 else between
        into += [(at, after), (after, at)]
    one = lax.ppermute(one, both, inside)
    two = lax.ppermute(two, both, between)
    rim = lax.ppermute(rim, both, across)
    return pl.pallas_call(
        functools.partial(step_kernel, sub_count, slots),
        out_shape=jax.ShapeDtypeStruct(populations.shape, jnp.float32),
        in_specs=[smem, smem, hbm, vmem, vmem, vmem],
        out_specs=vmem,
        scratch_shapes=[
            pltpu.VMEM((DIRS, HALVES, HOME + planes + BX + REACH + 4, LANES), jnp.float32),
            pltpu.VMEM((DIRS, HALVES, planes + 3 * 8, LANES), jnp.float32),
            pltpu.VMEM((DIRS, HALVES, planes + 3 * 8, LANES), jnp.float32),
            pltpu.SemaphoreType.DMA((HALVES,)),
        ],
        name="steps",
    )(old, new, populations, one, two, rim)


def solution(mesh):
    if mesh.shape["sub"] % 2:
        raise ValueError("odd sub")
    in_specs = (P(None, ("curve", "sub"), None), P(), P())
    out_specs = P(None, ("curve", "sub"), None)
    return jax.shard_map(shards, mesh=mesh, in_specs=in_specs, out_specs=out_specs, check_vma=False)
```

```python
import functools

import jax
import jax.numpy as jnp
import numpy as np
from jax import lax
from jax.experimental import pallas as pl
from jax.experimental.pallas import tpu as pltpu
from jax.sharding import PartitionSpec as P

BX = 16
BZ = 16
STEPS = 4
DIRS = 19
REACH = BX + STEPS
LANES = 128
HALVES = 2
PAD = 8
STRIP = 72
MID = 32

VELOCITY = np.array(
    [
        [0, 0, 0],
        [1, 0, 0],
        [1, 1, 0],
        [1, -1, 0],
        [1, 0, 1],
        [1, 0, -1],
        [-1, 0, 0],
        [-1, 1, 0],
        [-1, -1, 0],
        [-1, 0, 1],
        [-1, 0, -1],
        [0, 1, 0],
        [0, -1, 0],
        [0, 0, 1],
        [0, 0, -1],
        [0, 1, 1],
        [0, 1, -1],
        [0, -1, 1],
        [0, -1, -1],
    ]
)
tau_base = 0.6
smagorinsky = 0.17


def collide(h):
    def pair(first, second):
        return h[first] + h[second], h[first] - h[second]

    s_x, d_x = pair(1, 6)
    s_xyp, d_xyp = pair(2, 8)
    s_xym, d_xym = pair(3, 7)
    s_xzp, d_xzp = pair(4, 10)
    s_xzm, d_xzm = pair(5, 9)
    s_y, d_y = pair(11, 12)
    s_z, d_z = pair(13, 14)
    s_yzp, d_yzp = pair(15, 18)
    s_yzm, d_yzm = pair(16, 17)
    j_x = (d_x + d_x) + (d_xyp + d_xym) + (d_xzp + d_xzm)
    j_y = (d_y + d_y) + (d_xyp - d_xym) + (d_yzp + d_yzm)
    j_z = (d_z + d_z) + (d_xzp - d_xzm) + (d_yzp - d_yzm)
    t_xy, t_xz, t_yz = s_xyp + s_xym, s_xzp + s_xzm, s_yzp + s_yzm
    m_xy, m_xz, m_yz = s_xyp - s_xym, s_xzp - s_xzm, s_yzp - s_yzm
    ss_x, ss_y, ss_z = s_x + s_x, s_y + s_y, s_z + s_z
    yz_part = ss_y + t_yz
    m_xx = ss_x + (t_xy + t_xz)
    m_yy = yz_part + t_xy
    m_zz = ss_z + (t_xz + t_yz)
    rho36 = (12.0 * h[0] + ss_z) + (m_xx + yz_part)
    inverse = 1.0 / rho36
    k_u = 1.5 * inverse
    k_p = 2.25 * inverse
    u_x, u_y, u_z = j_x * k_u, j_y * k_u, j_z * k_u
    xx, yy, zz = u_x * u_x, u_y * u_y, u_z * u_z
    xy, xz, yz = u_x * u_y, u_x * u_z, u_y * u_z
    p_xx = m_xx * k_p - (xx + 0.75)
    p_yy = m_yy * k_p - (yy + 0.75)
    p_zz = m_zz * k_p - (zz + 0.75)
    p_xy = m_xy * k_p - xy
    p_xz = m_xz * k_p - xz
    p_yz = m_yz * k_p - yz
    off = p_xy * p_xy + p_xz * p_xz + p_yz * p_yz
    square = (p_xx * p_xx + p_yy * p_yy) + (p_zz * p_zz + (off + off))
    magnitude = jnp.sqrt(square)
    factor = 18.0 * np.sqrt(2.0) * smagorinsky * smagorinsky / 2.25
    inner = tau_base * tau_base + float(factor) * magnitude
    omega = 2.0 / (tau_base + inner * lax.rsqrt(inner))
    keep = 1.0 - omega
    gain = (omega * (1.0 / 36.0)) * rho36
    gain2 = gain + gain
    rest = gain - gain * ((2.0 / 3.0) * ((xx + yy) + zz))
    gain4 = gain2 + gain2
    a_x, a_y, a_z = gain2 * u_x, gain2 * u_y, gain2 * u_z
    b_x, b_y, b_z = a_x * u_x, a_y * u_y, a_z * u_z
    n_x, n_y, n_z = rest + b_x, rest + b_y, rest + b_z
    out = [None] * DIRS
    out[0] = keep * h[0] + rest

    def spread(first, second, even, odd):
        out[first] = keep * h[first] + (even + odd)
        out[second] = keep * h[second] + (even - odd)

    spread(1, 6, n_x, a_x)
    spread(11, 12, n_y, a_y)
    spread(13, 14, n_z, a_z)
    for plus, minus, base, cross, first, second in (
        ((2, 8), (3, 7), n_x + b_y, gain4 * xy, a_x, a_y),
        ((4, 10), (5, 9), n_x + b_z, gain4 * xz, a_x, a_z),
        ((15, 18), (16, 17), n_y + b_z, gain4 * yz, a_y, a_z),
    ):
        spread(*plus, base + cross, first + second)
        spread(*minus, base - cross, first - second)
    return out


def lane_sources(step_y, step_z):
    lane = lax.broadcasted_iota(jnp.int32, (8, LANES), 1)
    along_y = (lane - step_y * BZ) & (LANES - 1) & ~(BZ - 1)
    along_z = (lane - step_z) & (BZ - 1)
    return along_y | along_z


def moves():
    lane = lax.broadcasted_iota(jnp.int32, (8, LANES), 1)
    index = {}
    for step_y in (-1, 0, 1):
        for step_z in (-1, 1):
            index[step_y, step_z] = lane_sources(step_y, step_z)
    border = {1: lane < BZ, -1: lane >= LANES - BZ}
    return index, border


def shift_cross(lower, upper, direction, tables):
    index, border = tables
    step_y, step_z = int(VELOCITY[direction, 1]), int(VELOCITY[direction, 2])
    if step_z != 0:
        source = index[step_y, step_z]
        lower = jnp.take_along_axis(lower, source, axis=1, mode="promise_in_bounds")
        upper = jnp.take_along_axis(upper, source, axis=1, mode="promise_in_bounds")
    elif step_y != 0:
        lower = pltpu.roll(lower, (step_y * BZ) % LANES, 1)
        upper = pltpu.roll(upper, (step_y * BZ) % LANES, 1)
    if step_y != 0:
        edge = border[step_y]
        lower, upper = jnp.where(edge, upper, lower), jnp.where(edge, lower, upper)
    return lower, upper


def layout_of(sub_count, old_ref, new_ref, curve, sub):
    old_start, new_start = 0, 0
    for other in range(sub_count - 1):
        before = other < sub
        old_start += jnp.where(before, old_ref[other, curve], 0)
        new_start += jnp.where(before, new_ref[other, curve], 0)
    held_old = old_ref[sub, curve] * BX
    held_new = new_ref[sub, curve] * BX
    return held_old, held_new, (new_start - old_start) * BX


def pack_kernel(
    sub_count, old_hbm, new_hbm, pop_ref, one_ref, two_ref, far_ref, old_ref, new_ref, all_ref, sem,
):
    curve, sub = lax.axis_index("curve"), lax.axis_index("sub")
    loads = [pltpu.make_async_copy(old_hbm, old_ref, sem.at[0])]
    loads += [
        pltpu.make_async_copy(
            pop_ref.at[:, :, half * LANES : (half + 1) * LANES], all_ref.at[:, half], sem.at[1 + half]
        )
        for half in range(HALVES)
    ]
    for load in loads:
        load.start()
    for load in loads:
        load.wait()
    held_old = old_ref[sub, curve] * BX
    even = sub % 2 == 0
    right = held_old - REACH
    one_start = jnp.where(even, right, 0)
    two_start = jnp.where(even, 0, right)
    far_start = jnp.where(sub == 0, 0, held_old - STEPS)
    for target, start, count in (
        (one_ref, one_start, REACH),
        (two_ref, two_start, REACH),
        (far_ref, far_start, STEPS),
    ):
        for direction in range(DIRS):
            for half in range(HALVES):
                row = (direction * HALVES + half) * count
                target[row : row + count, :] = all_ref[direction, half, pl.ds(start, count), :]


def advance(source, target, rows, to, moving, tables):
    relaxed = []
    for row in rows:
        for half in range(HALVES):
            cells = []
            for direction in range(DIRS):
                at = row - int(VELOCITY[direction, 0]) if moving else row
                cells.append(source[direction, half, pl.ds(at, 8), :])
            relaxed.append(collide(cells))
    for at, row in enumerate(to):
        for direction in range(DIRS):
            lower, upper = shift_cross(
                relaxed[HALVES * at][direction], relaxed[HALVES * at + 1][direction], direction, tables
            )
            target[direction, 0, pl.ds(row, 8), :] = lower
            target[direction, 1, pl.ds(row, 8), :] = upper


def inner_kernel(
    sub_count, slots, old_ref, new_ref, pop_ref, out_ref, own_ref, cross_ref, edge_ref,
    first_ref, ping_ref, pong_ref, tile_ref, zero_ref, sem, out_sem,
):
    curve, sub = lax.axis_index("curve"), lax.axis_index("sub")
    loads = [
        pltpu.make_async_copy(
            pop_ref.at[:, :, half * LANES : (half + 1) * LANES],
            first_ref.at[:, half],
            sem.at[half],
        )
        for half in range(HALVES)
    ]
    for load in loads:
        load.start()
    held_old, held_new, offset = layout_of(sub_count, old_ref, new_ref, curve, sub)
    end = offset + held_new
    zero_ref[...] = jnp.zeros_like(zero_ref)

    def clear(slot):
        return pltpu.make_async_copy(
            zero_ref, out_ref.at[:, slot * BX : (slot + 1) * BX, :], out_sem.at[slot]
        )

    for slot in range(slots):

        @pl.when(slot * BX >= held_new)
        def _():
            clear(slot).start()

    for load in loads:
        load.wait()
    for direction in range(DIRS):
        for half in range(HALVES):
            own_ref[direction, half, :STEPS, :] = first_ref[direction, half, :STEPS, :]
            own_ref[direction, half, STEPS:, :] = first_ref[direction, half, pl.ds(held_old - STEPS, STEPS), :]
    tables = moves()
    last = held_old - STEPS - 1 + PAD

    def run(step, source, target):
        def body(pair, carry):
            row = pl.multiple_of(pair * 16, 16)
            top = row if step == 0 else row + PAD
            advance(source, target, [top, top + 8], [row + PAD, row + PAD + 8], step > 0, tables)
            return carry

        lax.fori_loop(0, held_old // 16, body, 0)
        for side, first in ((0, 6), (1, 1)):
            for at in range(5):
                for half in range(HALVES):
                    row = last if side else PAD + STEPS
                    cross_ref[((step * 2 + side) * 5 + at) * HALVES + half, :] = target[
                        first + at, half, row, :
                    ]

    run(0, first_ref, ping_ref)
    run(1, ping_ref, pong_ref)
    run(2, pong_ref, ping_ref)
    run(3, ping_ref, pong_ref)

    tiles = slots * BX // 8

    def write(tile):
        row = pl.multiple_of(jnp.clip(tile * 8 - offset, 0, (tiles - 1) * 8), 8)
        return pltpu.make_async_copy(
            tile_ref.at[:, tile * 8 : tile * 8 + 8, :], out_ref.at[:, pl.ds(row, 8), :], out_sem.at[slots + tile]
        )

    def kept(tile):
        inside = jnp.logical_and(tile * 8 >= offset, tile * 8 < end)
        return jnp.logical_and(inside, tile * 8 < held_old - 8)

    for tile in range(tiles):

        @pl.when(tile * 8 < held_old)
        def _():
            for direction in range(DIRS):
                row = PAD + tile * 8 - int(VELOCITY[direction, 0])
                for half in range(HALVES):
                    tile_ref[direction, tile * 8 : tile * 8 + 8, half * LANES : (half + 1) * LANES] = pong_ref[
                        direction, half, row : row + 8, :
                    ]

        if tile > 0:

            @pl.when(kept(tile))
            def _():
                write(tile).start()

    right = pl.multiple_of(held_old - 8, 8)
    for direction in range(DIRS):
        edge_ref[direction, 0:8, :] = tile_ref[direction, 0:8, :]
        edge_ref[direction, 8:16, :] = tile_ref[direction, pl.ds(right, 8), :]
    for slot in range(slots):

        @pl.when(slot * BX >= held_new)
        def _():
            clear(slot).wait()

    for tile in range(1, tiles):

        @pl.when(kept(tile))
        def _():
            write(tile).wait()


def tail_kernel(
    sub_count, old_ref, new_ref, own_ref, cross_ref, edge_ref, one_ref, two_ref, far_ref, _, out_ref,
    strip_ref, done_ref, sem,
):
    curve, sub = lax.axis_index("curve"), lax.axis_index("sub")
    held_old, held_new, offset = layout_of(sub_count, old_ref, new_ref, curve, sub)
    gained = offset + held_new - held_old
    lefts = jnp.where(offset == 0, 1, jnp.where(offset < 0, 3, 0))
    rights = jnp.where(gained == 0, 1, jnp.where(gained > 0, 3, 0))

    def place(source, count, start):
        for direction in range(DIRS):
            for half in range(HALVES):
                row = (direction * HALVES + half) * count
                strip_ref[0, direction, half, start : start + count, :] = source[row : row + count, :]

    even = sub % 2 == 0
    has_left, has_right = lefts > 0, rights > 0
    left_row, right_row = MID - STEPS - REACH, MID + 8 + STEPS

    @pl.when(jnp.logical_and(even, has_right))
    def _():
        place(one_ref, REACH, right_row)

    @pl.when(jnp.logical_and(jnp.logical_not(even), has_left))
    def _():
        place(one_ref, REACH, left_row)

    @pl.when(jnp.logical_and(jnp.logical_and(even, sub > 0), has_left))
    def _():
        place(two_ref, REACH, left_row)

    @pl.when(jnp.logical_and(jnp.logical_and(jnp.logical_not(even), sub < sub_count - 1), has_right))
    def _():
        place(two_ref, REACH, right_row)

    @pl.when(sub == 0)
    def _():
        place(far_ref, STEPS, MID - 2 * STEPS)

    @pl.when(sub == sub_count - 1)
    def _():
        place(far_ref, STEPS, right_row)

    for direction in range(DIRS):
        for half in range(HALVES):
            strip_ref[0, direction, half, MID - STEPS : MID, :] = own_ref[direction, half, :STEPS, :]
            strip_ref[0, direction, half, MID + 8 : MID + 8 + STEPS, :] = own_ref[direction, half, STEPS:, :]
    for step in range(STEPS):
        for side, first in ((0, 6), (1, 1)):
            for at in range(5):
                for half in range(HALVES):
                    row = MID + 7 if side else MID
                    strip_ref[step + 1, first + at, half, row, :] = cross_ref[
                        ((step * 2 + side) * 5 + at) * HALVES + half, :
                    ]
    tables = moves()
    work = lefts + rights

    def row_of(at):
        return pl.multiple_of(jnp.where(at < lefts, MID - 8 * (lefts - at), MID + 8 + 8 * (at - lefts)), 8)

    for step in range(STEPS):

        def body(pair, carry):
            rows = [row_of(2 * pair), row_of(2 * pair + 1)]
            advance(strip_ref.at[step], strip_ref.at[step + 1], rows, rows, step > 0, tables)
            return carry

        lax.fori_loop(0, (work + 1) // 2, body, 0)

    final = strip_ref.at[STEPS]
    plane = lax.broadcasted_iota(jnp.int32, (8, LANES), 0)

    def fetch(direction, half, row):
        row = row - int(VELOCITY[direction, 0])
        return final[direction, half, row : row + 8, :]

    def finish(side, merged, whole, row):
        for direction in range(DIRS):
            for half in range(HALVES):
                lanes = slice(half * LANES, (half + 1) * LANES)
                at, start = merged
                value = fetch(direction, half, start)
                inner = edge_ref[direction, side * 8 : side * 8 + 8, lanes]
                mine = plane < STEPS if side == 0 else plane >= STEPS
                done_ref[side, direction, at : at + 8, lanes] = jnp.where(mine, value, inner)
                for at, start in whole:
                    done_ref[side, direction, at : at + 8, lanes] = fetch(direction, half, start)

    def write(side, at, count, row):
        return pltpu.make_async_copy(
            done_ref.at[side, :, at : at + count, :], out_ref.at[:, pl.ds(pl.multiple_of(row, 8), count), :], sem.at[side]
        )

    left_low, right_high = MID - STEPS, MID + STEPS
    edge_row = held_old - 8 - offset
    left_moved, left_kept = write(0, 0, 24, 0), write(0, 16, 8, 0)
    right_moved, right_kept = write(1, 0, 24, edge_row), write(1, 0, 8, edge_row)

    @pl.when(lefts == 3)
    def _():
        finish(0, (16, left_low), [(0, left_low - 16), (8, left_low - 8)], 0)
        left_moved.start()

    @pl.when(lefts == 1)
    def _():
        finish(0, (16, left_low), [], 0)
        left_kept.start()

    @pl.when(rights == 3)
    def _():
        finish(1, (0, right_high), [(8, right_high + 8), (16, right_high + 16)], 0)
        right_moved.start()

    @pl.when(rights == 1)
    def _():
        finish(1, (0, right_high), [], 0)
        right_kept.start()

    for count, moved, kept in ((lefts, left_moved, left_kept), (rights, right_moved, right_kept)):

        @pl.when(count == 3)
        def _():
            moved.wait()

        @pl.when(count == 1)
        def _():
            kept.wait()


def shards(populations, count_old, count_new):
    curve_count, sub_count = lax.axis_size("curve"), lax.axis_size("sub")
    planes = populations.shape[1]
    slots = planes // BX
    total = curve_count * sub_count
    old, new = count_old.T, count_new.T
    smem = pl.BlockSpec(memory_space=pltpu.SMEM)
    hbm = pl.BlockSpec(memory_space=pltpu.HBM)
    vmem = pl.BlockSpec(memory_space=pltpu.VMEM)
    rows = DIRS * HALVES

    def local(*shape):
        return pltpu.VMEM(shape, jnp.float32)

    def near(value):
        return pltpu.with_memory_space_constraint(value, pltpu.VMEM)

    params = pltpu.CompilerParams(vmem_limit_bytes=32 << 20)

    populations, old, new = (pltpu.with_memory_space_constraint(value, pltpu.HBM) for value in (populations, old, new))
    one, two, rim = pl.pallas_call(
        functools.partial(pack_kernel, sub_count),
        out_shape=(local(rows * REACH, LANES), local(rows * REACH, LANES), local(rows * STEPS, LANES)),
        in_specs=[hbm, hbm, hbm],
        out_specs=(vmem, vmem, vmem),
        scratch_shapes=[
            pltpu.SMEM(old.shape, jnp.int32),
            pltpu.SMEM(old.shape, jnp.int32),
            pltpu.VMEM((DIRS, HALVES, planes, LANES), jnp.float32),
            pltpu.SemaphoreType.DMA((1 + HALVES,)),
        ],
        compiler_params=params,
        name="pack",
    )(old, new, populations)
    both = ("curve", "sub")
    inside = [(at, at ^ 1) for at in range(total)]
    between, across = [], []
    for at in range(1, total, 2):
        after = (at + 1) % total
        into = across if after % sub_count == 0 else between
        into += [(at, after), (after, at)]
    one = lax.ppermute(one, both, inside)
    two = lax.ppermute(two, both, between)
    rim = lax.ppermute(rim, both, across)
    state = pltpu.VMEM((DIRS, HALVES, planes + 2 * PAD, LANES), jnp.float32)
    result, own, cross, edge = pl.pallas_call(
        functools.partial(inner_kernel, sub_count, slots),
        out_shape=(
            jax.ShapeDtypeStruct(populations.shape, jnp.float32),
            local(DIRS, HALVES, 2 * STEPS, LANES),
            local(STEPS * 2 * 5 * HALVES, LANES),
            local(DIRS, 16, HALVES * LANES),
        ),
        in_specs=[smem, smem, hbm],
        out_specs=(hbm, vmem, vmem, vmem),
        scratch_shapes=[
            pltpu.VMEM((DIRS, HALVES, planes, LANES), jnp.float32),
            state,
            state,
            pltpu.VMEM(populations.shape, jnp.float32),
            pltpu.VMEM((DIRS, BX, HALVES * LANES), jnp.float32),
            pltpu.SemaphoreType.DMA((HALVES,)),
            pltpu.SemaphoreType.DMA((slots + slots * BX // 8,)),
        ],
        cost_estimate=pl.CostEstimate(flops=10**9, bytes_accessed=8 * 10**6, transcendentals=0),
        compiler_params=params,
        name="inner",
    )(old, new, populations)
    return pl.pallas_call(
        functools.partial(tail_kernel, sub_count),
        out_shape=jax.ShapeDtypeStruct(populations.shape, jnp.float32),
        in_specs=[smem, smem, vmem, vmem, vmem, vmem, vmem, vmem, hbm],
        out_specs=hbm,
        scratch_shapes=[
            pltpu.VMEM((STEPS + 1, DIRS, HALVES, STRIP, LANES), jnp.float32),
            pltpu.VMEM((2, DIRS, 24, HALVES * LANES), jnp.float32),
            pltpu.SemaphoreType.DMA((2,)),
        ],
        input_output_aliases={8: 0},
        compiler_params=params,
        name="tail",
    )(old, new, *map(near, (own, cross, edge, one, two, rim)), result)


def solution(mesh):
    if mesh.shape["sub"] % 2:
        raise ValueError("odd sub")
    in_specs = (P(None, ("curve", "sub"), None), P(), P())
    out_specs = P(None, ("curve", "sub"), None)
    return jax.shard_map(shards, mesh=mesh, in_specs=in_specs, out_specs=out_specs, check_vma=False)
```

```python
import functools

import jax
import jax.numpy as jnp
import numpy as np
from jax import lax
from jax.experimental import pallas as pl
from jax.experimental.pallas import tpu as pltpu
from jax.sharding import PartitionSpec as P

BX = 16
BZ = 16
STEPS = 4
DIRS = 19
REACH = BX + STEPS
LANES = 128
HALVES = 2
PAD = 8
STRIP = 40
LEFT_EDGE = 32

VELOCITY = np.array(
    [
        [0, 0, 0],
        [1, 0, 0],
        [1, 1, 0],
        [1, -1, 0],
        [1, 0, 1],
        [1, 0, -1],
        [-1, 0, 0],
        [-1, 1, 0],
        [-1, -1, 0],
        [-1, 0, 1],
        [-1, 0, -1],
        [0, 1, 0],
        [0, -1, 0],
        [0, 0, 1],
        [0, 0, -1],
        [0, 1, 1],
        [0, 1, -1],
        [0, -1, 1],
        [0, -1, -1],
    ]
)
tau_base = 0.6
smagorinsky = 0.17


def collide(h):
    def pair(first, second):
        return h[first] + h[second], h[first] - h[second]

    s_x, d_x = pair(1, 6)
    s_xyp, d_xyp = pair(2, 8)
    s_xym, d_xym = pair(3, 7)
    s_xzp, d_xzp = pair(4, 10)
    s_xzm, d_xzm = pair(5, 9)
    s_y, d_y = pair(11, 12)
    s_z, d_z = pair(13, 14)
    s_yzp, d_yzp = pair(15, 18)
    s_yzm, d_yzm = pair(16, 17)
    j_x = (d_x + d_x) + (d_xyp + d_xym) + (d_xzp + d_xzm)
    j_y = (d_y + d_y) + (d_xyp - d_xym) + (d_yzp + d_yzm)
    j_z = (d_z + d_z) + (d_xzp - d_xzm) + (d_yzp - d_yzm)
    t_xy, t_xz, t_yz = s_xyp + s_xym, s_xzp + s_xzm, s_yzp + s_yzm
    m_xy, m_xz, m_yz = s_xyp - s_xym, s_xzp - s_xzm, s_yzp - s_yzm
    ss_x, ss_y, ss_z = s_x + s_x, s_y + s_y, s_z + s_z
    yz_part = ss_y + t_yz
    m_xx = ss_x + (t_xy + t_xz)
    m_yy = yz_part + t_xy
    m_zz = ss_z + (t_xz + t_yz)
    rho36 = (12.0 * h[0] + ss_z) + (m_xx + yz_part)
    inverse = 1.0 / rho36
    k_u = 1.5 * inverse
    k_p = 2.25 * inverse
    u_x, u_y, u_z = j_x * k_u, j_y * k_u, j_z * k_u
    xx, yy, zz = u_x * u_x, u_y * u_y, u_z * u_z
    xy, xz, yz = u_x * u_y, u_x * u_z, u_y * u_z
    p_xx = m_xx * k_p - (xx + 0.75)
    p_yy = m_yy * k_p - (yy + 0.75)
    p_zz = m_zz * k_p - (zz + 0.75)
    p_xy = m_xy * k_p - xy
    p_xz = m_xz * k_p - xz
    p_yz = m_yz * k_p - yz
    off = p_xy * p_xy + p_xz * p_xz + p_yz * p_yz
    square = (p_xx * p_xx + p_yy * p_yy) + (p_zz * p_zz + (off + off))
    magnitude = jnp.sqrt(square)
    factor = 18.0 * np.sqrt(2.0) * smagorinsky * smagorinsky / 2.25
    inner = tau_base * tau_base + float(factor) * magnitude
    omega = 2.0 / (tau_base + inner * lax.rsqrt(inner))
    keep = 1.0 - omega
    gain = (omega * (1.0 / 36.0)) * rho36
    gain2 = gain + gain
    rest = gain - gain * ((2.0 / 3.0) * ((xx + yy) + zz))
    gain4 = gain2 + gain2
    a_x, a_y, a_z = gain2 * u_x, gain2 * u_y, gain2 * u_z
    b_x, b_y, b_z = a_x * u_x, a_y * u_y, a_z * u_z
    n_x, n_y, n_z = rest + b_x, rest + b_y, rest + b_z
    out = [None] * DIRS
    out[0] = keep * h[0] + rest

    def spread(first, second, even, odd):
        out[first] = keep * h[first] + (even + odd)
        out[second] = keep * h[second] + (even - odd)

    spread(1, 6, n_x, a_x)
    spread(11, 12, n_y, a_y)
    spread(13, 14, n_z, a_z)
    for plus, minus, base, cross, first, second in (
        ((2, 8), (3, 7), n_x + b_y, gain4 * xy, a_x, a_y),
        ((4, 10), (5, 9), n_x + b_z, gain4 * xz, a_x, a_z),
        ((15, 18), (16, 17), n_y + b_z, gain4 * yz, a_y, a_z),
    ):
        spread(*plus, base + cross, first + second)
        spread(*minus, base - cross, first - second)
    return out


def lane_sources(step_y, step_z):
    lane = lax.broadcasted_iota(jnp.int32, (8, LANES), 1)
    along_y = (lane - step_y * BZ) & (LANES - 1) & ~(BZ - 1)
    along_z = (lane - step_z) & (BZ - 1)
    return along_y | along_z


def moves():
    lane = lax.broadcasted_iota(jnp.int32, (8, LANES), 1)
    index = {}
    for step_y in (-1, 0, 1):
        for step_z in (-1, 1):
            index[step_y, step_z] = lane_sources(step_y, step_z)
    border = {1: lane < BZ, -1: lane >= LANES - BZ}
    return index, border


def shift_cross(lower, upper, direction, tables):
    index, border = tables
    step_y, step_z = int(VELOCITY[direction, 1]), int(VELOCITY[direction, 2])
    if step_z != 0:
        source = index[step_y, step_z]
        lower = jnp.take_along_axis(lower, source, axis=1, mode="promise_in_bounds")
        upper = jnp.take_along_axis(upper, source, axis=1, mode="promise_in_bounds")
    elif step_y != 0:
        lower = pltpu.roll(lower, (step_y * BZ) % LANES, 1)
        upper = pltpu.roll(upper, (step_y * BZ) % LANES, 1)
    if step_y != 0:
        edge = border[step_y]
        lower, upper = jnp.where(edge, upper, lower), jnp.where(edge, lower, upper)
    return lower, upper


def layout_of(sub_count, old_ref, new_ref, curve, sub):
    old_start, new_start = 0, 0
    for other in range(sub_count - 1):
        before = other < sub
        old_start += jnp.where(before, old_ref[other, curve], 0)
        new_start += jnp.where(before, new_ref[other, curve], 0)
    held_old = old_ref[sub, curve] * BX
    held_new = new_ref[sub, curve] * BX
    return held_old, held_new, (new_start - old_start) * BX


def pack_kernel(
    sub_count, old_hbm, new_hbm, pop_ref, one_ref, two_ref, far_ref, all_ref, info_ref, old_ref, new_ref, sem,
):
    curve, sub = lax.axis_index("curve"), lax.axis_index("sub")
    counts = [
        pltpu.make_async_copy(source, target, sem.at[at])
        for at, (source, target) in enumerate(((old_hbm, old_ref), (new_hbm, new_ref)))
    ]
    loads = [
        pltpu.make_async_copy(
            pop_ref.at[:, :, half * LANES : (half + 1) * LANES], all_ref.at[:, half], sem.at[2 + half]
        )
        for half in range(HALVES)
    ]
    for load in counts + loads:
        load.start()
    for load in counts:
        load.wait()
    held_old, held_new, offset = layout_of(sub_count, old_ref, new_ref, curve, sub)
    info_ref[0] = held_old
    info_ref[1] = held_new
    info_ref[2] = offset
    for load in loads:
        load.wait()
    even = sub % 2 == 0
    right = held_old - REACH
    one_start = jnp.where(even, right, 0)
    two_start = jnp.where(even, 0, right)
    far_start = jnp.where(sub == 0, 0, held_old - STEPS)
    for target, start, count in (
        (one_ref, one_start, REACH),
        (two_ref, two_start, REACH),
        (far_ref, far_start, STEPS),
    ):
        for direction in range(DIRS):
            for half in range(HALVES):
                row = (direction * HALVES + half) * count
                target[row : row + count, :] = all_ref[direction, half, pl.ds(start, count), :]


def fetch(source, row, moved):
    return [
        [source[direction, half, pl.ds(row - int(VELOCITY[direction, 0]) * moved, 8), :] for direction in range(DIRS)]
        for half in range(HALVES)
    ]


def shift(halves, tables):
    moved = [shift_cross(halves[0][direction], halves[1][direction], direction, tables) for direction in range(DIRS)]
    return [[pair[half] for pair in moved] for half in range(HALVES)]


def store(target, row, halves):
    for half in range(HALVES):
        for direction in range(DIRS):
            target[direction, half, pl.ds(row, 8), :] = halves[half][direction]


def inner_kernel(
    slots, info_ref, first_ref, out_ref, own_ref, cross_ref, edge_ref,
    ping_ref, pong_ref, raw_ref, tile_ref, zero_ref, out_sem,
):
    held_old, held_new, offset = info_ref[0], info_ref[1], info_ref[2]
    end = offset + held_new

    def clear(slot):
        return pltpu.make_async_copy(
            zero_ref, out_ref.at[:, slot * BX : (slot + 1) * BX, :], out_sem.at[slot]
        )

    @pl.when(held_new < slots * BX)
    def _():
        zero_ref[...] = jnp.zeros_like(zero_ref)

    for slot in range(slots):

        @pl.when(slot * BX >= held_new)
        def _():
            clear(slot).start()

    for direction in range(DIRS):
        for half in range(HALVES):
            own_ref[direction, half, :STEPS, :] = first_ref[direction, half, :STEPS, :]
            own_ref[direction, half, STEPS:, :] = first_ref[direction, half, pl.ds(held_old - STEPS, STEPS), :]
    tables = moves()
    last = held_old - STEPS - 1 + PAD
    pairs = held_old // 16

    def run(step, source, target):
        def settle(row):
            waiting = [fetch(raw_ref, at, 0) for at in (0, 8)]
            return [shift(halves, tables) for halves in waiting], (row, row + 8)

        def body(pair, carry):
            row = pl.multiple_of(pair * 16, 16)
            top = row if step == 0 else row + PAD
            values, rows = settle(pl.multiple_of(PAD + 16 * jnp.maximum(pair - 1, 0), 8))
            cells = [fetch(source, at, 1 if step else 0) for at in (top, top + 8)]
            relaxed = [[collide(half) for half in halves] for halves in cells]
            for at, halves in zip(rows, values):
                store(target, at, halves)
            for at, halves in zip((0, 8), relaxed):
                store(raw_ref, at, halves)
            return carry

        lax.fori_loop(0, pairs, body, 0)
        values, rows = settle(pl.multiple_of(PAD + 16 * (pairs - 1), 8))
        for at, halves in zip(rows, values):
            store(target, at, halves)
        for side, first in ((0, 6), (1, 1)):
            for at in range(5):
                for half in range(HALVES):
                    row = last if side else PAD + STEPS
                    cross_ref[((step * 2 + side) * 5 + at) * HALVES + half, :] = target[
                        first + at, half, row, :
                    ]

    run(0, first_ref, ping_ref)
    run(1, ping_ref, pong_ref)
    run(2, pong_ref, ping_ref)
    run(3, ping_ref, pong_ref)

    tiles = slots * BX // 8

    def write(tile):
        row = pl.multiple_of(jnp.clip(tile * 8 - offset, 0, (tiles - 1) * 8), 8)
        return pltpu.make_async_copy(
            tile_ref.at[:, tile * 8 : tile * 8 + 8, :], out_ref.at[:, pl.ds(row, 8), :], out_sem.at[slots + tile]
        )

    def kept(tile):
        inside = jnp.logical_and(tile * 8 >= offset, tile * 8 < end)
        return jnp.logical_and(inside, tile * 8 < held_old - 8)

    for tile in range(tiles):

        @pl.when(tile * 8 < held_old)
        def _():
            halves = fetch(pong_ref, PAD + tile * 8, 1)
            for direction in range(DIRS):
                for half in range(HALVES):
                    lanes = slice(half * LANES, (half + 1) * LANES)
                    tile_ref[direction, tile * 8 : tile * 8 + 8, lanes] = halves[half][direction]

        if tile > 0:

            @pl.when(kept(tile))
            def _():
                write(tile).start()

    right = pl.multiple_of(held_old - 8, 8)
    for direction in range(DIRS):
        edge_ref[direction, 0:8, :] = tile_ref[direction, 0:8, :]
        edge_ref[direction, 8:16, :] = tile_ref[direction, pl.ds(right, 8), :]
    for slot in range(slots):

        @pl.when(slot * BX >= held_new)
        def _():
            clear(slot).wait()

    for tile in range(1, tiles):

        @pl.when(kept(tile))
        def _():
            write(tile).wait()


def edge_kernel(sub_count, inside, info_ref, own_ref, cross_ref, edge_ref, *refs):
    if inside:
        near_ref, far_ref, (_, out_ref, strip_ref, done_ref, sem) = refs[0], None, refs[1:]
    else:
        near_ref, far_ref, _, out_ref, strip_ref, done_ref, sem = refs
    sub = lax.axis_index("sub")
    held_old, held_new, offset = info_ref[0], info_ref[1], info_ref[2]
    gained = offset + held_new - held_old
    even = sub % 2 == 0
    on_right = even if inside else jnp.logical_not(even)
    on_left = jnp.logical_not(on_right)
    extra = jnp.where(on_right, gained, -offset)
    heavy, light = extra > 0, extra == 0

    def place(source, count, first, used, start):
        for direction in range(DIRS):
            for half in range(HALVES):
                row = (direction * HALVES + half) * count + first
                strip_ref[0, direction, half, start : start + used, :] = source[row : row + used, :]

    def both(first, second):
        return jnp.logical_and(first, second)

    if far_ref is None:
        local = light
    else:
        outer = jnp.logical_or(sub == 0, sub == sub_count - 1)
        local = both(light, jnp.logical_not(outer))

        @pl.when(both(outer, on_left))
        def _():
            place(far_ref, STEPS, 0, STEPS, LEFT_EDGE - 2 * STEPS)

        @pl.when(both(outer, on_right))
        def _():
            place(far_ref, STEPS, 0, STEPS, PAD + STEPS)

    @pl.when(both(local, on_left))
    def _():
        place(near_ref, REACH, REACH - STEPS, STEPS, LEFT_EDGE - 2 * STEPS)

    @pl.when(both(local, on_right))
    def _():
        place(near_ref, REACH, 0, STEPS, PAD + STEPS)

    @pl.when(both(heavy, on_left))
    def _():
        place(near_ref, REACH, 0, REACH, PAD)

    @pl.when(both(heavy, on_right))
    def _():
        place(near_ref, REACH, 0, REACH, PAD + STEPS)

    @pl.when(on_left)
    def _():
        for direction in range(DIRS):
            for half in range(HALVES):
                strip_ref[0, direction, half, LEFT_EDGE - STEPS : LEFT_EDGE, :] = own_ref[direction, half, :STEPS, :]

    @pl.when(on_right)
    def _():
        for direction in range(DIRS):
            for half in range(HALVES):
                strip_ref[0, direction, half, PAD : PAD + STEPS, :] = own_ref[direction, half, STEPS:, :]

    for side, first, row, here in ((0, 6, LEFT_EDGE, on_left), (1, 1, PAD - 1, on_right)):

        @pl.when(here)
        def _():
            for step in range(STEPS):
                for at in range(5):
                    for half in range(HALVES):
                        strip_ref[step + 1, first + at, half, row, :] = cross_ref[
                            ((step * 2 + side) * 5 + at) * HALVES + half, :
                        ]

    tables = moves()

    def run(rows):
        def body(step, carry):
            moved = jnp.minimum(step, 1)
            cells = [fetch(strip_ref.at[step], row, moved) for row in rows]
            relaxed = [shift([collide(half) for half in halves], tables) for halves in cells]
            for row, halves in zip(rows, relaxed):
                store(strip_ref.at[step + 1], row, halves)
            return carry

        lax.fori_loop(0, STEPS, body, 0)

    @pl.when(heavy)
    def _():
        run([PAD, PAD + 8, PAD + 16])

    @pl.when(light)
    def _():
        run([pl.multiple_of(jnp.where(on_left, PAD + 16, PAD), 8)])

    final = strip_ref.at[STEPS]
    plane = lax.broadcasted_iota(jnp.int32, (8, LANES), 0)

    def finish(side, merged, whole, row):
        for at, start in [merged] + whole:
            halves = fetch(final, start, 1)
            for direction in range(DIRS):
                for half in range(HALVES):
                    lanes = slice(half * LANES, (half + 1) * LANES)
                    value = halves[half][direction]
                    if (at, start) == merged:
                        mine = plane < STEPS if side == 0 else plane >= STEPS
                        value = jnp.where(mine, value, edge_ref[direction, side * 8 : side * 8 + 8, lanes])
                    done_ref[direction, at : at + 8, lanes] = value
        count = 8 + 8 * len(whole)
        low = min(at for at, _ in [merged] + whole)
        copy = pltpu.make_async_copy(
            done_ref.at[:, low : low + count, :], out_ref.at[:, pl.ds(pl.multiple_of(row, 8), count), :], sem
        )
        copy.start()
        copy.wait()

    low, high = LEFT_EDGE - STEPS, PAD - STEPS
    edge_row = held_old - 8 - offset

    @pl.when(both(heavy, on_left))
    def _():
        finish(0, (16, low), [(0, low - 16), (8, low - 8)], 0)

    @pl.when(both(light, on_left))
    def _():
        finish(0, (16, low), [], 0)

    @pl.when(both(heavy, on_right))
    def _():
        finish(1, (0, high), [(8, high + 8), (16, high + 16)], edge_row)

    @pl.when(both(light, on_right))
    def _():
        finish(1, (0, high), [], edge_row)


def shards(populations, count_old, count_new):
    curve_count, sub_count = lax.axis_size("curve"), lax.axis_size("sub")
    planes = populations.shape[1]
    slots = planes // BX
    total = curve_count * sub_count
    old, new = count_old.T, count_new.T
    smem = pl.BlockSpec(memory_space=pltpu.SMEM)
    hbm = pl.BlockSpec(memory_space=pltpu.HBM)
    vmem = pl.BlockSpec(memory_space=pltpu.VMEM)
    rows = DIRS * HALVES
    whole = jax.ShapeDtypeStruct(populations.shape, jnp.float32)

    def local(*shape):
        return pltpu.VMEM(shape, jnp.float32)

    def near(value):
        return pltpu.with_memory_space_constraint(value, pltpu.VMEM)

    params = pltpu.CompilerParams(vmem_limit_bytes=32 << 20)
    populations, old, new = (
        pltpu.with_memory_space_constraint(value, pltpu.HBM) for value in (populations, old, new)
    )
    one, two, rim, cells, info = pl.pallas_call(
        functools.partial(pack_kernel, sub_count),
        out_shape=(
            local(rows * REACH, LANES),
            local(rows * REACH, LANES),
            local(rows * STEPS, LANES),
            local(DIRS, HALVES, planes, LANES),
            pltpu.SMEM((4,), jnp.int32),
        ),
        in_specs=[hbm, hbm, hbm],
        out_specs=(vmem, vmem, vmem, vmem, smem),
        scratch_shapes=[
            pltpu.SMEM(old.shape, jnp.int32),
            pltpu.SMEM(old.shape, jnp.int32),
            pltpu.SemaphoreType.DMA((2 + HALVES,)),
        ],
        compiler_params=params,
        name="pack",
    )(old, new, populations)
    info = pltpu.with_memory_space_constraint(info, pltpu.SMEM)
    cells = near(cells)
    both = ("curve", "sub")

    def everyone(pairs):
        busy = {source for source, _ in pairs}
        rest = [at for at in range(total) if at not in busy]
        return pairs + [(at, (at // sub_count ^ 1) * sub_count + at % sub_count) for at in rest]

    inside = [(at, at ^ 1) for at in range(total)]
    between, across = [], []
    for at in range(1, total, 2):
        after = (at + 1) % total
        into = across if after % sub_count == 0 else between
        into += [(at, after), (after, at)]
    one = lax.ppermute(one, both, inside)
    two = lax.ppermute(two, both, everyone(between))
    rim = lax.ppermute(rim, both, everyone(across))
    state = pltpu.VMEM((DIRS, HALVES, planes + 2 * PAD, LANES), jnp.float32)
    result, own, cross, edge = pl.pallas_call(
        functools.partial(inner_kernel, slots),
        out_shape=(
            whole,
            local(DIRS, HALVES, 2 * STEPS, LANES),
            local(STEPS * 2 * 5 * HALVES, LANES),
            local(DIRS, 16, HALVES * LANES),
        ),
        in_specs=[smem, vmem],
        out_specs=(hbm, vmem, vmem, vmem),
        scratch_shapes=[
            state,
            state,
            pltpu.VMEM((DIRS, HALVES, 16, LANES), jnp.float32),
            pltpu.VMEM(populations.shape, jnp.float32),
            pltpu.VMEM((DIRS, BX, HALVES * LANES), jnp.float32),
            pltpu.SemaphoreType.DMA((slots + slots * BX // 8,)),
        ],
        compiler_params=params,
        cost_estimate=pl.CostEstimate(flops=10**9, bytes_accessed=8 * 10**6, transcendentals=0),
        name="inner",
    )(info, cells)
    own, cross, edge = near(own), near(cross), near(edge)
    for at, received in enumerate(((one,), (two, rim))):
        result = pl.pallas_call(
            functools.partial(edge_kernel, sub_count, at == 0),
            out_shape=whole,
            in_specs=[smem, vmem, vmem, vmem] + [vmem] * len(received) + [hbm],
            out_specs=hbm,
            scratch_shapes=[
                pltpu.VMEM((STEPS + 1, DIRS, HALVES, STRIP, LANES), jnp.float32),
                pltpu.VMEM((DIRS, 24, HALVES * LANES), jnp.float32),
                pltpu.SemaphoreType.DMA,
            ],
            input_output_aliases={4 + len(received): 0},
            compiler_params=params,
            cost_estimate=pl.CostEstimate(flops=10**8, bytes_accessed=10**6, transcendentals=0),
            name="edges",
        )(info, own, cross, edge, *map(near, received), result)
    return result


def solution(mesh):
    if mesh.shape["sub"] % 2 or mesh.shape["curve"] % 2:
        raise ValueError("odd mesh")
    in_specs = (P(None, ("curve", "sub"), None), P(), P())
    out_specs = P(None, ("curve", "sub"), None)
    return jax.shard_map(shards, mesh=mesh, in_specs=in_specs, out_specs=out_specs, check_vma=False)
```

```python
import functools

import jax
import jax.numpy as jnp
import numpy as np
from jax import lax
from jax.experimental import pallas as pl
from jax.experimental.pallas import tpu as pltpu
from jax.sharding import PartitionSpec as P

BX = 16
BZ = 16
STEPS = 4
DIRS = 19
REACH = BX + STEPS
LANES = 128
HALVES = 2
PAD = 8
STRIP = 72
MID = 32
SPLIT = 10
TOWARD = {0: (6, 7, 8, 9, 10), 1: (1, 2, 3, 4, 5)}
LEVEL = (0, 11, 12, 13, 14, 15, 16, 17, 18)

VELOCITY = np.array(
    [
        [0, 0, 0],
        [1, 0, 0],
        [1, 1, 0],
        [1, -1, 0],
        [1, 0, 1],
        [1, 0, -1],
        [-1, 0, 0],
        [-1, 1, 0],
        [-1, -1, 0],
        [-1, 0, 1],
        [-1, 0, -1],
        [0, 1, 0],
        [0, -1, 0],
        [0, 0, 1],
        [0, 0, -1],
        [0, 1, 1],
        [0, 1, -1],
        [0, -1, 1],
        [0, -1, -1],
    ]
)
tau_base = 0.6
smagorinsky = 0.17


def collide(h):
    def pair(first, second):
        return h[first] + h[second], h[first] - h[second]

    s_x, d_x = pair(1, 6)
    s_xyp, d_xyp = pair(2, 8)
    s_xym, d_xym = pair(3, 7)
    s_xzp, d_xzp = pair(4, 10)
    s_xzm, d_xzm = pair(5, 9)
    s_y, d_y = pair(11, 12)
    s_z, d_z = pair(13, 14)
    s_yzp, d_yzp = pair(15, 18)
    s_yzm, d_yzm = pair(16, 17)
    j_x = (d_x + d_x) + (d_xyp + d_xym) + (d_xzp + d_xzm)
    j_y = (d_y + d_y) + (d_xyp - d_xym) + (d_yzp + d_yzm)
    j_z = (d_z + d_z) + (d_xzp - d_xzm) + (d_yzp - d_yzm)
    t_xy, t_xz, t_yz = s_xyp + s_xym, s_xzp + s_xzm, s_yzp + s_yzm
    m_xy, m_xz, m_yz = s_xyp - s_xym, s_xzp - s_xzm, s_yzp - s_yzm
    ss_x, ss_y, ss_z = s_x + s_x, s_y + s_y, s_z + s_z
    yz_part = ss_y + t_yz
    m_xx = ss_x + (t_xy + t_xz)
    m_yy = yz_part + t_xy
    m_zz = ss_z + (t_xz + t_yz)
    rho36 = (12.0 * h[0] + ss_z) + (m_xx + yz_part)
    inverse = 1.0 / rho36
    k_u = 1.5 * inverse
    k_p = 2.25 * inverse
    u_x, u_y, u_z = j_x * k_u, j_y * k_u, j_z * k_u
    xx, yy, zz = u_x * u_x, u_y * u_y, u_z * u_z
    xy, xz, yz = u_x * u_y, u_x * u_z, u_y * u_z
    p_xx = m_xx * k_p - (xx + 0.75)
    p_yy = m_yy * k_p - (yy + 0.75)
    p_zz = m_zz * k_p - (zz + 0.75)
    p_xy = m_xy * k_p - xy
    p_xz = m_xz * k_p - xz
    p_yz = m_yz * k_p - yz
    off = p_xy * p_xy + p_xz * p_xz + p_yz * p_yz
    square = (p_xx * p_xx + p_yy * p_yy) + (p_zz * p_zz + (off + off))
    magnitude = jnp.sqrt(square)
    factor = 18.0 * np.sqrt(2.0) * smagorinsky * smagorinsky / 2.25
    inner = tau_base * tau_base + float(factor) * magnitude
    omega = 2.0 / (tau_base + inner * lax.rsqrt(inner))
    keep = 1.0 - omega
    gain = (omega * (1.0 / 36.0)) * rho36
    gain2 = gain + gain
    rest = gain - gain * ((2.0 / 3.0) * ((xx + yy) + zz))
    gain4 = gain2 + gain2
    a_x, a_y, a_z = gain2 * u_x, gain2 * u_y, gain2 * u_z
    b_x, b_y, b_z = a_x * u_x, a_y * u_y, a_z * u_z
    n_x, n_y, n_z = rest + b_x, rest + b_y, rest + b_z
    out = [None] * DIRS
    out[0] = keep * h[0] + rest

    def spread(first, second, even, odd):
        out[first] = keep * h[first] + (even + odd)
        out[second] = keep * h[second] + (even - odd)

    spread(1, 6, n_x, a_x)
    spread(11, 12, n_y, a_y)
    spread(13, 14, n_z, a_z)
    for plus, minus, base, cross, first, second in (
        ((2, 8), (3, 7), n_x + b_y, gain4 * xy, a_x, a_y),
        ((4, 10), (5, 9), n_x + b_z, gain4 * xz, a_x, a_z),
        ((15, 18), (16, 17), n_y + b_z, gain4 * yz, a_y, a_z),
    ):
        spread(*plus, base + cross, first + second)
        spread(*minus, base - cross, first - second)
    return out


def lane_sources(step_y, step_z):
    lane = lax.broadcasted_iota(jnp.int32, (8, LANES), 1)
    along_y = (lane - step_y * BZ) & (LANES - 1) & ~(BZ - 1)
    along_z = (lane - step_z) & (BZ - 1)
    return along_y | along_z


def moves():
    lane = lax.broadcasted_iota(jnp.int32, (8, LANES), 1)
    index = {}
    for step_y in (-1, 0, 1):
        for step_z in (-1, 1):
            index[step_y, step_z] = lane_sources(step_y, step_z)
    border = {1: lane < BZ, -1: lane >= LANES - BZ}
    return index, border


def shift_cross(lower, upper, direction, tables):
    index, border = tables
    step_y, step_z = int(VELOCITY[direction, 1]), int(VELOCITY[direction, 2])
    if step_z != 0:
        source = index[step_y, step_z]
        lower = jnp.take_along_axis(lower, source, axis=1, mode="promise_in_bounds")
        upper = jnp.take_along_axis(upper, source, axis=1, mode="promise_in_bounds")
    elif step_y != 0:
        lower = pltpu.roll(lower, (step_y * BZ) % LANES, 1)
        upper = pltpu.roll(upper, (step_y * BZ) % LANES, 1)
    if step_y != 0:
        edge = border[step_y]
        lower, upper = jnp.where(edge, upper, lower), jnp.where(edge, lower, upper)
    return lower, upper


def layout_of(sub_count, old_ref, new_ref, curve, sub):
    old_start, new_start = 0, 0
    for other in range(sub_count - 1):
        before = other < sub
        old_start += jnp.where(before, old_ref[other, curve], 0)
        new_start += jnp.where(before, new_ref[other, curve], 0)
    held_old = old_ref[sub, curve] * BX
    held_new = new_ref[sub, curve] * BX
    return held_old, held_new, (new_start - old_start) * BX


def pack_kernel(
    sub_count, old_hbm, new_hbm, pop_ref, one_ref, more_ref, two_ref, all_ref, info_ref, old_ref, new_ref, sem,
):
    curve, sub = lax.axis_index("curve"), lax.axis_index("sub")
    counts = [
        pltpu.make_async_copy(source, target, sem.at[at])
        for at, (source, target) in enumerate(((old_hbm, old_ref), (new_hbm, new_ref)))
    ]
    loads = [
        pltpu.make_async_copy(
            pop_ref.at[:, :, half * LANES : (half + 1) * LANES], all_ref.at[:, half], sem.at[2 + half]
        )
        for half in range(HALVES)
    ]
    for load in counts + loads:
        load.start()
    for load in counts:
        load.wait()
    held_old, held_new, offset = layout_of(sub_count, old_ref, new_ref, curve, sub)
    info_ref[0] = held_old
    info_ref[1] = held_new
    info_ref[2] = offset
    for load in loads:
        load.wait()
    even = sub % 2 == 0
    right = held_old - REACH
    one_start = jnp.where(even, right, 0)
    two_start = jnp.where(even, 0, right)
    for target, start, count in (
        (one_ref, one_start, SPLIT),
        (more_ref, one_start + SPLIT, REACH - SPLIT),
        (two_ref, two_start, REACH),
    ):
        for direction in range(DIRS):
            for half in range(HALVES):
                row = (direction * HALVES + half) * count
                target[row : row + count, :] = all_ref[direction, half, pl.ds(start, count), :]


def fetch(source, row, moved):
    return [
        [source[direction, half, pl.ds(row - int(VELOCITY[direction, 0]) * moved, 8), :] for direction in range(DIRS)]
        for half in range(HALVES)
    ]


def shift(halves, tables):
    moved = [shift_cross(halves[0][direction], halves[1][direction], direction, tables) for direction in range(DIRS)]
    return [[pair[half] for pair in moved] for half in range(HALVES)]


def store(target, row, halves):
    for half in range(HALVES):
        for direction in range(DIRS):
            target[direction, half, pl.ds(row, 8), :] = halves[half][direction]


def rim_parts(side):
    parts, row = [], 0
    for half in range(HALVES):
        for directions, count in ((TOWARD[side], 4), (LEVEL, 3), (TOWARD[1 - side], 2)):
            for direction in directions:
                parts.append((direction, half, row, 0 if side == 0 else STEPS - count, count))
                row += count
    return parts


RIM = sum(part[-1] for part in rim_parts(0))


def rim_kernel(sub_count, info_ref, cells_ref, far_ref):
    sub = lax.axis_index("sub")
    tables = moves()

    def send(side, row):
        relaxed = shift([collide(half) for half in fetch(cells_ref, row, 0)], tables)
        for direction, half, at, first, count in rim_parts(side):
            first += STEPS * side
            far_ref[at : at + count, :] = relaxed[half][direction][first : first + count, :]

    @pl.when(sub == 0)
    def _():
        send(0, 0)

    @pl.when(sub == sub_count - 1)
    def _():
        send(1, pl.multiple_of(info_ref[0] - 8, 8))


def inner_kernel(
    slots, info_ref, first_ref, out_ref, own_ref, next_ref, cross_ref, edge_ref,
    ping_ref, pong_ref, raw_ref, tile_ref, zero_ref, out_sem,
):
    held_old, held_new, offset = info_ref[0], info_ref[1], info_ref[2]
    end = offset + held_new

    def clear(slot):
        return pltpu.make_async_copy(
            zero_ref, out_ref.at[:, slot * BX : (slot + 1) * BX, :], out_sem.at[slot]
        )

    @pl.when(held_new < slots * BX)
    def _():
        zero_ref[...] = jnp.zeros_like(zero_ref)

    for slot in range(slots):

        @pl.when(slot * BX >= held_new)
        def _():
            clear(slot).start()

    for direction in range(DIRS):
        for half in range(HALVES):
            own_ref[direction, half, :STEPS, :] = first_ref[direction, half, :STEPS, :]
            own_ref[direction, half, STEPS:, :] = first_ref[direction, half, pl.ds(held_old - STEPS, STEPS), :]
    tables = moves()
    last = held_old - STEPS - 1 + PAD
    pairs = held_old // 16

    def run(step, source, target):
        def settle(row):
            waiting = [fetch(raw_ref, at, 0) for at in (0, 8)]
            return [shift(halves, tables) for halves in waiting], (row, row + 8)

        def body(pair, carry):
            row = pl.multiple_of(pair * 16, 16)
            top = row if step == 0 else row + PAD
            values, rows = settle(pl.multiple_of(PAD + 16 * jnp.maximum(pair - 1, 0), 8))
            cells = [fetch(source, at, 1 if step else 0) for at in (top, top + 8)]
            relaxed = [[collide(half) for half in halves] for halves in cells]
            for at, halves in zip(rows, values):
                store(target, at, halves)
            for at, halves in zip((0, 8), relaxed):
                store(raw_ref, at, halves)
            return carry

        lax.fori_loop(0, pairs, body, 0)
        values, rows = settle(pl.multiple_of(PAD + 16 * (pairs - 1), 8))
        for at, halves in zip(rows, values):
            store(target, at, halves)
        for side, first in ((0, 6), (1, 1)):
            for at in range(5):
                for half in range(HALVES):
                    row = last if side else PAD + STEPS
                    cross_ref[((step * 2 + side) * 5 + at) * HALVES + half, :] = target[
                        first + at, half, row, :
                    ]

    run(0, first_ref, ping_ref)
    for direction in range(DIRS):
        for half in range(HALVES):
            next_ref[direction, half, :STEPS, :] = ping_ref[direction, half, PAD : PAD + STEPS, :]
            next_ref[direction, half, STEPS:, :] = ping_ref[direction, half, pl.ds(last + 1, STEPS), :]
    run(1, ping_ref, pong_ref)
    run(2, pong_ref, ping_ref)
    run(3, ping_ref, pong_ref)

    tiles = slots * BX // 8

    def write(tile):
        row = pl.multiple_of(jnp.clip(tile * 8 - offset, 0, (tiles - 1) * 8), 8)
        return pltpu.make_async_copy(
            tile_ref.at[:, tile * 8 : tile * 8 + 8, :], out_ref.at[:, pl.ds(row, 8), :], out_sem.at[slots + tile]
        )

    def kept(tile):
        inside = jnp.logical_and(tile * 8 >= offset, tile * 8 < end)
        return jnp.logical_and(inside, tile * 8 < held_old - 8)

    for tile in range(tiles):

        @pl.when(tile * 8 < held_old)
        def _():
            halves = fetch(pong_ref, PAD + tile * 8, 1)
            for direction in range(DIRS):
                for half in range(HALVES):
                    lanes = slice(half * LANES, (half + 1) * LANES)
                    tile_ref[direction, tile * 8 : tile * 8 + 8, lanes] = halves[half][direction]

        if tile > 0:

            @pl.when(kept(tile))
            def _():
                write(tile).start()

    right = pl.multiple_of(held_old - 8, 8)
    for direction in range(DIRS):
        edge_ref[direction, 0:8, :] = tile_ref[direction, 0:8, :]
        edge_ref[direction, 8:16, :] = tile_ref[direction, pl.ds(right, 8), :]
    for slot in range(slots):

        @pl.when(slot * BX >= held_new)
        def _():
            clear(slot).wait()

    for tile in range(1, tiles):

        @pl.when(kept(tile))
        def _():
            write(tile).wait()


def both(first, second):
    return jnp.logical_and(first, second)


def finish(side, source, merged, whole, row, edge_ref, out_ref, done_ref, sem):
    plane = lax.broadcasted_iota(jnp.int32, (8, LANES), 0)
    mine = plane < STEPS if side == 0 else plane >= STEPS
    for at, start in [merged] + whole:
        halves = fetch(source, start, 1)
        for direction in range(DIRS):
            for half in range(HALVES):
                lanes = slice(half * LANES, (half + 1) * LANES)
                value = halves[half][direction]
                if (at, start) == merged:
                    value = jnp.where(mine, value, edge_ref[direction, side * 8 : side * 8 + 8, lanes])
                done_ref[direction, at : at + 8, lanes] = value
    low, count = min(at for at, _ in [merged] + whole), 8 + 8 * len(whole)
    copy = pltpu.make_async_copy(
        done_ref.at[:, low : low + count, :], out_ref.at[:, pl.ds(pl.multiple_of(row, 8), count), :], sem
    )
    copy.start()
    return copy


def outer_kernel(
    sub_count, info_ref, next_ref, cross_ref, edge_ref, far_ref, _, out_ref, strip_ref, done_ref, sem,
):
    sub = lax.axis_index("sub")
    held_old, offset = info_ref[0], info_ref[2]

    def end(side):
        beside, own, border = (PAD, PAD + STEPS, PAD + 8) if side == 0 else (PAD + STEPS, PAD, PAD - 1)
        for direction, half, at, first, count in rim_parts(1 - side):
            strip_ref[0, direction, half, beside + first : beside + first + count, :] = far_ref[at : at + count, :]
        for direction in range(DIRS):
            for half in range(HALVES):
                strip_ref[0, direction, half, own : own + STEPS, :] = next_ref[
                    direction, half, side * STEPS : (side + 1) * STEPS, :
                ]
        for step in range(STEPS):
            for at in range(5):
                for half in range(HALVES):
                    strip_ref[step, TOWARD[side][at], half, border, :] = cross_ref[
                        ((step * 2 + side) * 5 + at) * HALVES + half, :
                    ]
        tables = moves()

        def body(step, carry):
            relaxed = shift([collide(half) for half in fetch(strip_ref.at[step], PAD, 1)], tables)
            store(strip_ref.at[step + 1], PAD, relaxed)
            return carry

        lax.fori_loop(0, STEPS - 1, body, 0)
        start, row = (PAD + STEPS, 0) if side == 0 else (PAD - STEPS, held_old - 8 - offset)
        finish(side, strip_ref.at[STEPS - 1], (0, start), [], row, edge_ref, out_ref, done_ref, sem).wait()

    @pl.when(sub == 0)
    def _():
        end(0)

    @pl.when(sub == sub_count - 1)
    def _():
        end(1)


def tail_kernel(
    sub_count, info_ref, own_ref, cross_ref, edge_ref, one_ref, more_ref, two_ref, _, out_ref,
    strip_ref, left_ref, right_ref, sem,
):
    sub = lax.axis_index("sub")
    held_old, held_new, offset = info_ref[0], info_ref[1], info_ref[2]
    gained = offset + held_new - held_old
    lefts = jnp.where(offset == 0, 1, jnp.where(offset < 0, 3, 0))
    rights = jnp.where(gained == 0, 1, jnp.where(gained > 0, 3, 0))
    lefts = jnp.where(sub == 0, 0, lefts)
    rights = jnp.where(sub == sub_count - 1, 0, rights)
    even = sub % 2 == 0
    odd = jnp.logical_not(even)

    def place(source, count, first, used, start):
        for direction in range(DIRS):
            for half in range(HALVES):
                row = (direction * HALVES + half) * count + first
                strip_ref[0, direction, half, start : start + used, :] = source[row : row + used, :]

    low, high, rest = MID - STEPS - REACH, MID + 8 + STEPS, REACH - SPLIT

    for here, count, start, light in ((odd, lefts, low, False), (even, rights, high, True)):

        @pl.when(both(here, count == 3))
        def _():
            place(one_ref, SPLIT, 0, SPLIT, start)
            place(more_ref, rest, 0, rest, start + SPLIT)

        @pl.when(both(here, count == 1))
        def _():
            if light:
                place(one_ref, SPLIT, 0, STEPS, start)
            else:
                place(more_ref, rest, rest - STEPS, STEPS, start + REACH - STEPS)

    for here, count, start, first in ((even, lefts, low, REACH - STEPS), (odd, rights, high, 0)):

        @pl.when(both(here, count == 3))
        def _():
            place(two_ref, REACH, 0, REACH, start)

        @pl.when(both(here, count == 1))
        def _():
            place(two_ref, REACH, first, STEPS, start + first)

    for side, count, start, border in ((0, lefts, MID - STEPS, MID), (1, rights, MID + 8, MID + 7)):

        @pl.when(count > 0)
        def _():
            for direction in range(DIRS):
                for half in range(HALVES):
                    strip_ref[0, direction, half, start : start + STEPS, :] = own_ref[
                        direction, half, side * STEPS : (side + 1) * STEPS, :
                    ]
            for step in range(STEPS):
                for at in range(5):
                    for half in range(HALVES):
                        strip_ref[step + 1, TOWARD[side][at], half, border, :] = cross_ref[
                            ((step * 2 + side) * 5 + at) * HALVES + half, :
                        ]

    tables = moves()
    work = lefts + rights

    def row_of(at):
        return pl.multiple_of(jnp.where(at < lefts, MID - 8 * (lefts - at), MID + 8 + 8 * (at - lefts)), 8)

    for groups in (1, 2, 3, 4, 6):

        @pl.when(work == groups)
        def _():
            rows = [row_of(at) for at in range(groups)]

            def body(step, carry):
                moved = jnp.minimum(step, 1)
                cells = [fetch(strip_ref.at[step], row, moved) for row in rows]
                relaxed = [shift([collide(half) for half in halves], tables) for halves in cells]
                for row, halves in zip(rows, relaxed):
                    store(strip_ref.at[step + 1], row, halves)
                return carry

            lax.fori_loop(0, STEPS, body, 0)

    final = strip_ref.at[STEPS]
    first, last = MID - STEPS, MID + STEPS
    row = held_old - 8 - offset
    ends = (
        (lefts, 0, (16, first), [(0, first - 16), (8, first - 8)], 0, left_ref),
        (rights, 1, (0, last), [(8, last + 8), (16, last + 16)], row, right_ref),
    )
    for count, side, merged, whole, to, done in ends:
        for amount, used in ((3, whole), (1, [])):

            @pl.when(count == amount)
            def _():
                finish(side, final, merged, used, to, edge_ref, out_ref, done, sem.at[side])

    for count, side, merged, whole, to, done in ends:
        for amount in (3, 1):

            @pl.when(count == amount)
            def _():
                size = 8 * amount
                start = 0 if amount == 3 else merged[0]
                pltpu.make_async_copy(
                    done.at[:, start : start + size, :],
                    out_ref.at[:, pl.ds(pl.multiple_of(to, 8), size), :],
                    sem.at[side],
                ).wait()


def shards(populations, count_old, count_new):
    curve_count, sub_count = lax.axis_size("curve"), lax.axis_size("sub")
    planes = populations.shape[1]
    slots = planes // BX
    total = curve_count * sub_count
    old, new = count_old.T, count_new.T
    smem = pl.BlockSpec(memory_space=pltpu.SMEM)
    hbm = pl.BlockSpec(memory_space=pltpu.HBM)
    vmem = pl.BlockSpec(memory_space=pltpu.VMEM)
    rows = DIRS * HALVES
    whole = jax.ShapeDtypeStruct(populations.shape, jnp.float32)

    def local(*shape):
        return pltpu.VMEM(shape, jnp.float32)

    def near(value):
        return pltpu.with_memory_space_constraint(value, pltpu.VMEM)

    params = pltpu.CompilerParams(vmem_limit_bytes=32 << 20)
    populations, old, new = (
        pltpu.with_memory_space_constraint(value, pltpu.HBM) for value in (populations, old, new)
    )
    one, more, two, cells, info = pl.pallas_call(
        functools.partial(pack_kernel, sub_count),
        out_shape=(
            local(rows * SPLIT, LANES),
            local(rows * (REACH - SPLIT), LANES),
            local(rows * REACH, LANES),
            local(DIRS, HALVES, planes, LANES),
            pltpu.SMEM((4,), jnp.int32),
        ),
        in_specs=[hbm, hbm, hbm],
        out_specs=(vmem, vmem, vmem, vmem, smem),
        scratch_shapes=[
            pltpu.SMEM(old.shape, jnp.int32),
            pltpu.SMEM(old.shape, jnp.int32),
            pltpu.SemaphoreType.DMA((2 + HALVES,)),
        ],
        compiler_params=params,
        name="pack",
    )(old, new, populations)
    info = pltpu.with_memory_space_constraint(info, pltpu.SMEM)
    cells = near(cells)
    axes = ("curve", "sub")

    def everyone(pairs):
        busy = {source for source, _ in pairs}
        rest = [at for at in range(total) if at not in busy]
        return pairs + [(at, (at // sub_count ^ 1) * sub_count + at % sub_count) for at in rest]

    def send(value, pairs):
        return lax.ppermute(value, axes, pairs)

    inside = [(at, at ^ 1) for at in range(total)]
    between, across = [], []
    for at in range(1, total, 2):
        after = (at + 1) % total
        into = across if after % sub_count == 0 else between
        into += [(at, after), (after, at)]
    one = send(one, inside)
    two = send(two, everyone(between))
    rim = pl.pallas_call(
        functools.partial(rim_kernel, sub_count),
        out_shape=local(RIM, LANES),
        in_specs=[smem, vmem],
        out_specs=vmem,
        compiler_params=params,
        name="rim",
    )(info, cells)
    rim = send(rim, everyone(across))
    more = send(more, inside)
    state = pltpu.VMEM((DIRS, HALVES, planes + 2 * PAD, LANES), jnp.float32)
    result, own, following, cross, edge = pl.pallas_call(
        functools.partial(inner_kernel, slots),
        out_shape=(
            whole,
            local(DIRS, HALVES, 2 * STEPS, LANES),
            local(DIRS, HALVES, 2 * STEPS, LANES),
            local(STEPS * 2 * 5 * HALVES, LANES),
            local(DIRS, 16, HALVES * LANES),
        ),
        in_specs=[smem, vmem],
        out_specs=(hbm, vmem, vmem, vmem, vmem),
        scratch_shapes=[
            state,
            state,
            pltpu.VMEM((DIRS, HALVES, 16, LANES), jnp.float32),
            pltpu.VMEM(populations.shape, jnp.float32),
            pltpu.VMEM((DIRS, BX, HALVES * LANES), jnp.float32),
            pltpu.SemaphoreType.DMA((slots + slots * BX // 8,)),
        ],
        compiler_params=params,
        cost_estimate=pl.CostEstimate(flops=10**9, bytes_accessed=8 * 10**6, transcendentals=0),
        name="inner",
    )(info, cells)
    own, following, cross, edge = map(near, (own, following, cross, edge))
    result = pl.pallas_call(
        functools.partial(outer_kernel, sub_count),
        out_shape=whole,
        in_specs=[smem, vmem, vmem, vmem, vmem, hbm],
        out_specs=hbm,
        scratch_shapes=[
            pltpu.VMEM((STEPS, DIRS, HALVES, 3 * PAD, LANES), jnp.float32),
            pltpu.VMEM((DIRS, 8, HALVES * LANES), jnp.float32),
            pltpu.SemaphoreType.DMA,
        ],
        input_output_aliases={5: 0},
        compiler_params=params,
        cost_estimate=pl.CostEstimate(flops=10**8, bytes_accessed=10**6, transcendentals=0),
        name="outer",
    )(info, following, cross, edge, near(rim), result)
    return pl.pallas_call(
        functools.partial(tail_kernel, sub_count),
        out_shape=whole,
        in_specs=[smem] + [vmem] * 6 + [hbm],
        out_specs=hbm,
        scratch_shapes=[
            pltpu.VMEM((STEPS + 1, DIRS, HALVES, STRIP, LANES), jnp.float32),
            pltpu.VMEM((DIRS, 24, HALVES * LANES), jnp.float32),
            pltpu.VMEM((DIRS, 24, HALVES * LANES), jnp.float32),
            pltpu.SemaphoreType.DMA((2,)),
        ],
        input_output_aliases={7: 0},
        compiler_params=params,
        cost_estimate=pl.CostEstimate(flops=10**8, bytes_accessed=10**6, transcendentals=0),
        name="tail",
    )(info, own, cross, edge, near(one), near(more), near(two), result)


def solution(mesh):
    if mesh.shape["sub"] % 2 or mesh.shape["curve"] % 2:
        raise ValueError("odd mesh")
    in_specs = (P(None, ("curve", "sub"), None), P(), P())
    out_specs = P(None, ("curve", "sub"), None)
    return jax.shard_map(shards, mesh=mesh, in_specs=in_specs, out_specs=out_specs, check_vma=False)
```

```python
import functools

import jax
import jax.numpy as jnp
import numpy as np
from jax import lax
from jax.experimental import pallas as pl
from jax.experimental.pallas import tpu as pltpu
from jax.sharding import PartitionSpec as P

BX = 16
BZ = 16
STEPS = 4
DIRS = 19
REACH = BX + STEPS
LANES = 128
HALVES = 2
PAD = 8
STRIP = 72
MID = 32
SPLIT = 12
TOWARD = {0: (6, 7, 8, 9, 10), 1: (1, 2, 3, 4, 5)}
LEVEL = (0, 11, 12, 13, 14, 15, 16, 17, 18)

VELOCITY = np.array(
    [
        [0, 0, 0],
        [1, 0, 0],
        [1, 1, 0],
        [1, -1, 0],
        [1, 0, 1],
        [1, 0, -1],
        [-1, 0, 0],
        [-1, 1, 0],
        [-1, -1, 0],
        [-1, 0, 1],
        [-1, 0, -1],
        [0, 1, 0],
        [0, -1, 0],
        [0, 0, 1],
        [0, 0, -1],
        [0, 1, 1],
        [0, 1, -1],
        [0, -1, 1],
        [0, -1, -1],
    ]
)
tau_base = 0.6
smagorinsky = 0.17


def collide(h):
    def pair(first, second):
        return h[first] + h[second], h[first] - h[second]

    s_x, d_x = pair(1, 6)
    s_xyp, d_xyp = pair(2, 8)
    s_xym, d_xym = pair(3, 7)
    s_xzp, d_xzp = pair(4, 10)
    s_xzm, d_xzm = pair(5, 9)
    s_y, d_y = pair(11, 12)
    s_z, d_z = pair(13, 14)
    s_yzp, d_yzp = pair(15, 18)
    s_yzm, d_yzm = pair(16, 17)
    j_x = (d_x + d_x) + (d_xyp + d_xym) + (d_xzp + d_xzm)
    j_y = (d_y + d_y) + (d_xyp - d_xym) + (d_yzp + d_yzm)
    j_z = (d_z + d_z) + (d_xzp - d_xzm) + (d_yzp - d_yzm)
    t_xy, t_xz, t_yz = s_xyp + s_xym, s_xzp + s_xzm, s_yzp + s_yzm
    m_xy, m_xz, m_yz = s_xyp - s_xym, s_xzp - s_xzm, s_yzp - s_yzm
    ss_x, ss_y, ss_z = s_x + s_x, s_y + s_y, s_z + s_z
    yz_part = ss_y + t_yz
    m_xx = ss_x + (t_xy + t_xz)
    m_yy = yz_part + t_xy
    m_zz = ss_z + (t_xz + t_yz)
    rho36 = (12.0 * h[0] + ss_z) + (m_xx + yz_part)
    inverse = 1.0 / rho36
    k_u = 1.5 * inverse
    k_p = 2.25 * inverse
    u_x, u_y, u_z = j_x * k_u, j_y * k_u, j_z * k_u
    xx, yy, zz = u_x * u_x, u_y * u_y, u_z * u_z
    xy, xz, yz = u_x * u_y, u_x * u_z, u_y * u_z
    p_xx = m_xx * k_p - (xx + 0.75)
    p_yy = m_yy * k_p - (yy + 0.75)
    p_zz = m_zz * k_p - (zz + 0.75)
    p_xy = m_xy * k_p - xy
    p_xz = m_xz * k_p - xz
    p_yz = m_yz * k_p - yz
    off = p_xy * p_xy + p_xz * p_xz + p_yz * p_yz
    square = (p_xx * p_xx + p_yy * p_yy) + (p_zz * p_zz + (off + off))
    magnitude = jnp.sqrt(square)
    factor = 18.0 * np.sqrt(2.0) * smagorinsky * smagorinsky / 2.25
    inner = tau_base * tau_base + float(factor) * magnitude
    omega = 2.0 / (tau_base + inner * lax.rsqrt(inner))
    keep = 1.0 - omega
    gain = (omega * (1.0 / 36.0)) * rho36
    gain2 = gain + gain
    rest = gain - gain * ((2.0 / 3.0) * ((xx + yy) + zz))
    gain4 = gain2 + gain2
    a_x, a_y, a_z = gain2 * u_x, gain2 * u_y, gain2 * u_z
    b_x, b_y, b_z = a_x * u_x, a_y * u_y, a_z * u_z
    n_x, n_y, n_z = rest + b_x, rest + b_y, rest + b_z
    out = [None] * DIRS
    out[0] = keep * h[0] + rest

    def spread(first, second, even, odd):
        out[first] = keep * h[first] + (even + odd)
        out[second] = keep * h[second] + (even - odd)

    spread(1, 6, n_x, a_x)
    spread(11, 12, n_y, a_y)
    spread(13, 14, n_z, a_z)
    for plus, minus, base, cross, first, second in (
        ((2, 8), (3, 7), n_x + b_y, gain4 * xy, a_x, a_y),
        ((4, 10), (5, 9), n_x + b_z, gain4 * xz, a_x, a_z),
        ((15, 18), (16, 17), n_y + b_z, gain4 * yz, a_y, a_z),
    ):
        spread(*plus, base + cross, first + second)
        spread(*minus, base - cross, first - second)
    return out


def lane_sources(step_y, step_z):
    lane = lax.broadcasted_iota(jnp.int32, (8, LANES), 1)
    along_y = (lane - step_y * BZ) & (LANES - 1) & ~(BZ - 1)
    along_z = (lane - step_z) & (BZ - 1)
    return along_y | along_z


def moves():
    lane = lax.broadcasted_iota(jnp.int32, (8, LANES), 1)
    index = {}
    for step_y in (-1, 0, 1):
        for step_z in (-1, 1):
            index[step_y, step_z] = lane_sources(step_y, step_z)
    border = {1: lane < BZ, -1: lane >= LANES - BZ}
    return index, border


def shift_cross(lower, upper, direction, tables):
    index, border = tables
    step_y, step_z = int(VELOCITY[direction, 1]), int(VELOCITY[direction, 2])
    if step_z != 0:
        source = index[step_y, step_z]
        lower = jnp.take_along_axis(lower, source, axis=1, mode="promise_in_bounds")
        upper = jnp.take_along_axis(upper, source, axis=1, mode="promise_in_bounds")
    elif step_y != 0:
        lower = pltpu.roll(lower, (step_y * BZ) % LANES, 1)
        upper = pltpu.roll(upper, (step_y * BZ) % LANES, 1)
    if step_y != 0:
        edge = border[step_y]
        lower, upper = jnp.where(edge, upper, lower), jnp.where(edge, lower, upper)
    return lower, upper


def layout_of(sub_count, old_ref, new_ref, curve, sub):
    old_start, new_start = 0, 0
    for other in range(sub_count - 1):
        before = other < sub
        old_start += jnp.where(before, old_ref[other, curve], 0)
        new_start += jnp.where(before, new_ref[other, curve], 0)
    held_old = old_ref[sub, curve] * BX
    held_new = new_ref[sub, curve] * BX
    return held_old, held_new, (new_start - old_start) * BX


def pack_kernel(
    sub_count, old_hbm, new_hbm, pop_ref, one_ref, more_ref, two_ref, all_ref, info_ref, old_ref, new_ref, sem,
):
    curve, sub = lax.axis_index("curve"), lax.axis_index("sub")
    counts = [
        pltpu.make_async_copy(source, target, sem.at[at])
        for at, (source, target) in enumerate(((old_hbm, old_ref), (new_hbm, new_ref)))
    ]
    loads = [
        pltpu.make_async_copy(
            pop_ref.at[:, :, half * LANES : (half + 1) * LANES], all_ref.at[:, half], sem.at[2 + half]
        )
        for half in range(HALVES)
    ]
    for load in counts + loads:
        load.start()
    for load in counts:
        load.wait()
    held_old, held_new, offset = layout_of(sub_count, old_ref, new_ref, curve, sub)
    info_ref[0] = held_old
    info_ref[1] = held_new
    info_ref[2] = offset
    for load in loads:
        load.wait()
    even = sub % 2 == 0
    right = held_old - REACH
    one_start = jnp.where(even, right, 0)
    two_start = jnp.where(even, 0, right)
    for target, start, count in (
        (one_ref, one_start, SPLIT),
        (more_ref, one_start + SPLIT, REACH - SPLIT),
        (two_ref, two_start, REACH),
    ):
        for direction in range(DIRS):
            for half in range(HALVES):
                row = (direction * HALVES + half) * count
                target[row : row + count, :] = all_ref[direction, half, pl.ds(start, count), :]


def fetch(source, row, moved):
    return [
        [source[direction, half, pl.ds(row - int(VELOCITY[direction, 0]) * moved, 8), :] for direction in range(DIRS)]
        for half in range(HALVES)
    ]


def shift(halves, tables):
    moved = [shift_cross(halves[0][direction], halves[1][direction], direction, tables) for direction in range(DIRS)]
    return [[pair[half] for pair in moved] for half in range(HALVES)]


def store(target, row, halves):
    for half in range(HALVES):
        for direction in range(DIRS):
            target[direction, half, pl.ds(row, 8), :] = halves[half][direction]


def rim_parts(side):
    parts, row = [], 0
    for half in range(HALVES):
        for directions, count in ((TOWARD[side], 4), (LEVEL, 3), (TOWARD[1 - side], 2)):
            for direction in directions:
                parts.append((direction, half, row, 0 if side == 0 else STEPS - count, count))
                row += count
    return parts


RIM = sum(part[-1] for part in rim_parts(0))


def rim_kernel(sub_count, info_ref, cells_ref, far_ref):
    sub = lax.axis_index("sub")
    tables = moves()

    def send(side, row):
        relaxed = shift([collide(half) for half in fetch(cells_ref, row, 0)], tables)
        for direction, half, at, first, count in rim_parts(side):
            first += STEPS * side
            far_ref[at : at + count, :] = relaxed[half][direction][first : first + count, :]

    @pl.when(sub == 0)
    def _():
        send(0, 0)

    @pl.when(sub == sub_count - 1)
    def _():
        send(1, pl.multiple_of(info_ref[0] - 8, 8))


def inner_kernel(
    slots, info_ref, first_ref, out_ref, own_ref, next_ref, cross_ref, edge_ref,
    ping_ref, pong_ref, raw_ref, tile_ref, zero_ref, out_sem,
):
    held_old, held_new, offset = info_ref[0], info_ref[1], info_ref[2]
    end = offset + held_new

    def clear(slot):
        return pltpu.make_async_copy(
            zero_ref, out_ref.at[:, slot * BX : (slot + 1) * BX, :], out_sem.at[slot]
        )

    @pl.when(held_new < slots * BX)
    def _():
        zero_ref[...] = jnp.zeros_like(zero_ref)

    for slot in range(slots):

        @pl.when(slot * BX >= held_new)
        def _():
            clear(slot).start()

    for direction in range(DIRS):
        for half in range(HALVES):
            own_ref[direction, half, :STEPS, :] = first_ref[direction, half, :STEPS, :]
            own_ref[direction, half, STEPS:, :] = first_ref[direction, half, pl.ds(held_old - STEPS, STEPS), :]
    tables = moves()
    last = held_old - STEPS - 1 + PAD
    pairs = held_old // 16

    def run(step, source, target):
        def settle(row):
            waiting = [fetch(raw_ref, at, 0) for at in (0, 8)]
            return [shift(halves, tables) for halves in waiting], (row, row + 8)

        def body(pair, carry):
            row = pl.multiple_of(pair * 16, 16)
            top = row if step == 0 else row + PAD
            values, rows = settle(pl.multiple_of(PAD + 16 * jnp.maximum(pair - 1, 0), 8))
            cells = [fetch(source, at, 1 if step else 0) for at in (top, top + 8)]
            relaxed = [[collide(half) for half in halves] for halves in cells]
            for at, halves in zip(rows, values):
                store(target, at, halves)
            for at, halves in zip((0, 8), relaxed):
                store(raw_ref, at, halves)
            return carry

        lax.fori_loop(0, pairs, body, 0)
        values, rows = settle(pl.multiple_of(PAD + 16 * (pairs - 1), 8))
        for at, halves in zip(rows, values):
            store(target, at, halves)
        for side, first in ((0, 6), (1, 1)):
            for at in range(5):
                for half in range(HALVES):
                    row = last if side else PAD + STEPS
                    cross_ref[((step * 2 + side) * 5 + at) * HALVES + half, :] = target[
                        first + at, half, row, :
                    ]

    run(0, first_ref, ping_ref)
    for direction in range(DIRS):
        for half in range(HALVES):
            next_ref[direction, half, :STEPS, :] = ping_ref[direction, half, PAD : PAD + STEPS, :]
            next_ref[direction, half, STEPS:, :] = ping_ref[direction, half, pl.ds(last + 1, STEPS), :]
    run(1, ping_ref, pong_ref)
    run(2, pong_ref, ping_ref)
    run(3, ping_ref, pong_ref)

    tiles = slots * BX // 8

    def write(tile):
        row = pl.multiple_of(jnp.clip(tile * 8 - offset, 0, (tiles - 1) * 8), 8)
        return pltpu.make_async_copy(
            tile_ref.at[:, tile * 8 : tile * 8 + 8, :], out_ref.at[:, pl.ds(row, 8), :], out_sem.at[slots + tile]
        )

    def kept(tile):
        inside = jnp.logical_and(tile * 8 >= offset, tile * 8 < end)
        return jnp.logical_and(inside, tile * 8 < held_old - 8)

    for tile in range(tiles):

        @pl.when(tile * 8 < held_old)
        def _():
            halves = fetch(pong_ref, PAD + tile * 8, 1)
            for direction in range(DIRS):
                for half in range(HALVES):
                    lanes = slice(half * LANES, (half + 1) * LANES)
                    tile_ref[direction, tile * 8 : tile * 8 + 8, lanes] = halves[half][direction]

        if tile > 0:

            @pl.when(kept(tile))
            def _():
                write(tile).start()

    right = pl.multiple_of(held_old - 8, 8)
    for direction in range(DIRS):
        edge_ref[direction, 0:8, :] = tile_ref[direction, 0:8, :]
        edge_ref[direction, 8:16, :] = tile_ref[direction, pl.ds(right, 8), :]
    for slot in range(slots):

        @pl.when(slot * BX >= held_new)
        def _():
            clear(slot).wait()

    for tile in range(1, tiles):

        @pl.when(kept(tile))
        def _():
            write(tile).wait()


def both(first, second):
    return jnp.logical_and(first, second)


def finish(side, source, merged, whole, row, edge_ref, out_ref, done_ref, sem):
    plane = lax.broadcasted_iota(jnp.int32, (8, LANES), 0)
    mine = plane < STEPS if side == 0 else plane >= STEPS
    for at, start in [merged] + whole:
        halves = fetch(source, start, 1)
        for direction in range(DIRS):
            for half in range(HALVES):
                lanes = slice(half * LANES, (half + 1) * LANES)
                value = halves[half][direction]
                if (at, start) == merged:
                    value = jnp.where(mine, value, edge_ref[direction, side * 8 : side * 8 + 8, lanes])
                done_ref[direction, at : at + 8, lanes] = value
    low, count = min(at for at, _ in [merged] + whole), 8 + 8 * len(whole)
    copy = pltpu.make_async_copy(
        done_ref.at[:, low : low + count, :], out_ref.at[:, pl.ds(pl.multiple_of(row, 8), count), :], sem
    )
    copy.start()
    return copy


def tail_kernel(
    sub_count, info_ref, own_ref, next_ref, cross_ref, edge_ref, one_ref, also_ref, more_ref, two_ref, far_ref, _, out_ref,
    strip_ref, first_raw_ref, second_raw_ref, left_ref, right_ref, sem,
):
    sub = lax.axis_index("sub")
    held_old, held_new, offset = info_ref[0], info_ref[1], info_ref[2]
    gained = offset + held_new - held_old
    lefts = jnp.where(offset == 0, 1, jnp.where(offset < 0, 3, 0))
    rights = jnp.where(gained == 0, 1, jnp.where(gained > 0, 3, 0))
    outer_left, outer_right = sub == 0, sub == sub_count - 1
    inner_left, inner_right = jnp.logical_not(outer_left), jnp.logical_not(outer_right)
    outer = jnp.logical_or(outer_left, outer_right)
    even = sub % 2 == 0
    odd = jnp.logical_not(even)

    def place(source, count, first, used, start):
        for direction in range(DIRS):
            for half in range(HALVES):
                row = (direction * HALVES + half) * count + first
                strip_ref[0, direction, half, start : start + used, :] = source[row : row + used, :]

    low, high, rest = MID - STEPS - REACH, MID + 8 + STEPS, REACH - SPLIT

    later = sub // 2 % 2 == 1
    sooner = jnp.logical_not(later)

    for source, when in ((one_ref, sooner), (also_ref, later)):
        for here, count, start, right in ((odd, lefts, low, False), (even, rights, high, True)):

            @pl.when(both(both(here, when), count == 3))
            def _():
                place(source, SPLIT, 0, SPLIT, start)

            if right:

                @pl.when(both(both(here, when), count == 1))
                def _():
                    place(source, SPLIT, 0, STEPS, start)

    for here, count, start, right in ((odd, lefts, low, False), (even, rights, high, True)):

        @pl.when(both(here, count == 3))
        def _():
            place(more_ref, rest, 0, rest, start + SPLIT)

        if not right:

            @pl.when(both(here, count == 1))
            def _():
                place(more_ref, rest, rest - STEPS, STEPS, start + REACH - STEPS)

    for here, count, start, first in (
        (both(even, inner_left), lefts, low, REACH - STEPS),
        (both(odd, inner_right), rights, high, 0),
    ):

        @pl.when(both(here, count == 3))
        def _():
            place(two_ref, REACH, 0, REACH, start)

        @pl.when(both(here, count == 1))
        def _():
            place(two_ref, REACH, first, STEPS, start + first)

    for side, here in ((0, outer_left), (1, outer_right)):

        @pl.when(here)
        def _():
            beside, own = (MID - 8, MID - STEPS) if side == 0 else (MID + 8 + STEPS, MID + 8)
            for direction, half, at, first, count in rim_parts(1 - side):
                strip_ref[1, direction, half, beside + first : beside + first + count, :] = far_ref[at : at + count, :]
            for direction in range(DIRS):
                for half in range(HALVES):
                    strip_ref[1, direction, half, own : own + STEPS, :] = next_ref[
                        direction, half, side * STEPS : (side + 1) * STEPS, :
                    ]

    for side, count, start, border in ((0, lefts, MID - STEPS, MID), (1, rights, MID + 8, MID + 7)):

        @pl.when(count > 0)
        def _():
            for direction in range(DIRS):
                for half in range(HALVES):
                    strip_ref[0, direction, half, start : start + STEPS, :] = own_ref[
                        direction, half, side * STEPS : (side + 1) * STEPS, :
                    ]
            for step in range(STEPS):
                for at in range(5):
                    for half in range(HALVES):
                        strip_ref[step + 1, TOWARD[side][at], half, border, :] = cross_ref[
                            ((step * 2 + side) * 5 + at) * HALVES + half, :
                        ]

    tables = moves()
    swap = jnp.where(outer, outer_left, lefts < rights)
    firsts, seconds = jnp.where(swap, rights, lefts), jnp.where(swap, lefts, rights)
    skip = jnp.where(outer, 1, 0)
    left_row, right_row = MID - 8 * lefts, MID + 8
    first_row = pl.multiple_of(jnp.where(swap, right_row, left_row), 8)
    second_row = pl.multiple_of(jnp.where(swap, left_row, right_row), 8)

    def plain(row, count, start):
        rows = [row + 8 * at for at in range(count)]

        def body(step, carry):
            cells = [fetch(strip_ref.at[step], at, jnp.minimum(step, 1)) for at in rows]
            relaxed = [shift([collide(half) for half in halves], tables) for halves in cells]
            for at, halves in zip(rows, relaxed):
                store(strip_ref.at[step + 1], at, halves)
            return carry

        lax.fori_loop(start, STEPS, body, 0)

    def staggered(first_count, second_count):
        one = (first_raw_ref, [first_row + 8 * at for at in range(first_count)])
        two = (second_raw_ref, [second_row + 8 * at for at in range(second_count)])

        def half_step(step, collided, settled, into):
            raw_out, rows = collided
            raw_in, to = settled
            waiting = [fetch(raw_in, 8 * at, 0) for at in range(len(to))]
            cells = [fetch(strip_ref.at[step], at, jnp.minimum(step, 1)) for at in rows]
            moved = [shift(halves, tables) for halves in waiting]
            relaxed = [[collide(half) for half in halves] for halves in cells]
            for at, halves in zip(to, moved):
                store(strip_ref.at[into], at, halves)
            for at, halves in enumerate(relaxed):
                store(raw_out, 8 * at, halves)

        def body(step, carry):
            half_step(step, one, two, jnp.where(step <= skip, STEPS + 1, step))
            half_step(step, two, one, step + 1)
            return carry

        lax.fori_loop(0, STEPS, body, 0)
        raw, rows = two
        moved = [shift(fetch(raw, 8 * at, 0), tables) for at in range(len(rows))]
        for at, halves in zip(rows, moved):
            store(strip_ref.at[STEPS], at, halves)

    for first_count, second_count in ((1, 1), (3, 1), (3, 3)):

        @pl.when(both(firsts == first_count, seconds == second_count))
        def _():
            staggered(first_count, second_count)

    for count in (1, 3):

        @pl.when(both(firsts == count, seconds == 0))
        def _():
            plain(first_row, count, 0)

    @pl.when(both(firsts == 0, seconds == 1))
    def _():
        plain(second_row, 1, skip)

    final = strip_ref.at[STEPS]
    first, last = MID - STEPS, MID + STEPS
    row = held_old - 8 - offset
    ends = (
        (lefts, 0, (16, first), [(0, first - 16), (8, first - 8)], 0, left_ref),
        (rights, 1, (0, last), [(8, last + 8), (16, last + 16)], row, right_ref),
    )
    for count, side, merged, whole, to, done in ends:
        for amount, used in ((3, whole), (1, [])):

            @pl.when(count == amount)
            def _():
                finish(side, final, merged, used, to, edge_ref, out_ref, done, sem.at[side])

    for count, side, merged, whole, to, done in ends:
        for amount in (3, 1):

            @pl.when(count == amount)
            def _():
                size = 8 * amount
                start = 0 if amount == 3 else merged[0]
                pltpu.make_async_copy(
                    done.at[:, start : start + size, :],
                    out_ref.at[:, pl.ds(pl.multiple_of(to, 8), size), :],
                    sem.at[side],
                ).wait()


def shards(populations, count_old, count_new):
    curve_count, sub_count = lax.axis_size("curve"), lax.axis_size("sub")
    planes = populations.shape[1]
    slots = planes // BX
    total = curve_count * sub_count
    old, new = count_old.T, count_new.T
    smem = pl.BlockSpec(memory_space=pltpu.SMEM)
    hbm = pl.BlockSpec(memory_space=pltpu.HBM)
    vmem = pl.BlockSpec(memory_space=pltpu.VMEM)
    rows = DIRS * HALVES
    whole = jax.ShapeDtypeStruct(populations.shape, jnp.float32)

    def local(*shape):
        return pltpu.VMEM(shape, jnp.float32)

    def near(value):
        return pltpu.with_memory_space_constraint(value, pltpu.VMEM)

    params = pltpu.CompilerParams(vmem_limit_bytes=32 << 20)
    populations, old, new = (
        pltpu.with_memory_space_constraint(value, pltpu.HBM) for value in (populations, old, new)
    )
    one, more, two, cells, info = pl.pallas_call(
        functools.partial(pack_kernel, sub_count),
        out_shape=(
            local(rows * SPLIT, LANES),
            local(rows * (REACH - SPLIT), LANES),
            local(rows * REACH, LANES),
            local(DIRS, HALVES, planes, LANES),
            pltpu.SMEM((4,), jnp.int32),
        ),
        in_specs=[hbm, hbm, hbm],
        out_specs=(vmem, vmem, vmem, vmem, smem),
        scratch_shapes=[
            pltpu.SMEM(old.shape, jnp.int32),
            pltpu.SMEM(old.shape, jnp.int32),
            pltpu.SemaphoreType.DMA((2 + HALVES,)),
        ],
        compiler_params=params,
        name="pack",
    )(old, new, populations)
    info = pltpu.with_memory_space_constraint(info, pltpu.SMEM)
    cells = near(cells)
    axes = ("curve", "sub")

    def everyone(pairs):
        busy = {source for source, _ in pairs}
        rest = [at for at in range(total) if at not in busy]
        return pairs + [(at, (at // sub_count ^ 1) * sub_count + at % sub_count) for at in rest]

    def send(value, pairs):
        return lax.ppermute(value, axes, pairs)

    inside = [(at, at ^ 1) for at in range(total)]
    between, across = [], []
    for at in range(1, total, 2):
        after = (at + 1) % total
        into = across if after % sub_count == 0 else between
        into += [(at, after), (after, at)]
    sooner = [(at, beside) for at, beside in inside if at % sub_count // 2 % 2 == 0]
    later = [(at, beside) for at, beside in inside if at % sub_count // 2 % 2 == 1]
    ends = one
    one = send(ends, everyone(sooner))
    two = send(two, everyone(between))
    also = send(ends, everyone(later))
    rim = pl.pallas_call(
        functools.partial(rim_kernel, sub_count),
        out_shape=local(RIM, LANES),
        in_specs=[smem, vmem],
        out_specs=vmem,
        compiler_params=params,
        name="rim",
    )(info, cells)
    rim = send(rim, everyone(across))
    more = send(more, inside)
    state = pltpu.VMEM((DIRS, HALVES, planes + 2 * PAD, LANES), jnp.float32)
    result, own, following, cross, edge = pl.pallas_call(
        functools.partial(inner_kernel, slots),
        out_shape=(
            whole,
            local(DIRS, HALVES, 2 * STEPS, LANES),
            local(DIRS, HALVES, 2 * STEPS, LANES),
            local(STEPS * 2 * 5 * HALVES, LANES),
            local(DIRS, 16, HALVES * LANES),
        ),
        in_specs=[smem, vmem],
        out_specs=(hbm, vmem, vmem, vmem, vmem),
        scratch_shapes=[
            state,
            state,
            pltpu.VMEM((DIRS, HALVES, 16, LANES), jnp.float32),
            pltpu.VMEM(populations.shape, jnp.float32),
            pltpu.VMEM((DIRS, BX, HALVES * LANES), jnp.float32),
            pltpu.SemaphoreType.DMA((slots + slots * BX // 8,)),
        ],
        compiler_params=params,
        cost_estimate=pl.CostEstimate(flops=10**9, bytes_accessed=8 * 10**6, transcendentals=0),
        name="inner",
    )(info, cells)
    own, following, cross, edge = map(near, (own, following, cross, edge))
    return pl.pallas_call(
        functools.partial(tail_kernel, sub_count),
        out_shape=whole,
        in_specs=[smem] + [vmem] * 9 + [hbm],
        out_specs=hbm,
        scratch_shapes=[
            pltpu.VMEM((STEPS + 2, DIRS, HALVES, STRIP, LANES), jnp.float32),
            pltpu.VMEM((DIRS, HALVES, 24, LANES), jnp.float32),
            pltpu.VMEM((DIRS, HALVES, 24, LANES), jnp.float32),
            pltpu.VMEM((DIRS, 24, HALVES * LANES), jnp.float32),
            pltpu.VMEM((DIRS, 24, HALVES * LANES), jnp.float32),
            pltpu.SemaphoreType.DMA((2,)),
        ],
        input_output_aliases={10: 0},
        compiler_params=params,
        cost_estimate=pl.CostEstimate(flops=10**8, bytes_accessed=10**6, transcendentals=0),
        name="tail",
    )(info, own, following, cross, edge, *map(near, (one, also, more, two, rim)), result)


def solution(mesh):
    if mesh.shape["sub"] % 2 or mesh.shape["curve"] % 2:
        raise ValueError("odd mesh")
    in_specs = (P(None, ("curve", "sub"), None), P(), P())
    out_specs = P(None, ("curve", "sub"), None)
    return jax.shard_map(shards, mesh=mesh, in_specs=in_specs, out_specs=out_specs, check_vma=False)
```

```python
import functools

import jax
import jax.numpy as jnp
import numpy as np
from jax import lax
from jax.experimental import pallas as pl
from jax.experimental.pallas import tpu as pltpu
from jax.sharding import PartitionSpec as P

BX = 16
BZ = 16
STEPS = 4
DIRS = 19
LANES = 128
HALVES = 2
PAD = 8
STRIP = 40
EDGE = 24
SPLIT = 11
TOWARD = {0: (6, 7, 8, 9, 10), 1: (1, 2, 3, 4, 5)}
LEVEL = (0, 11, 12, 13, 14, 15, 16, 17, 18)

VELOCITY = np.array(
    [
        [0, 0, 0],
        [1, 0, 0],
        [1, 1, 0],
        [1, -1, 0],
        [1, 0, 1],
        [1, 0, -1],
        [-1, 0, 0],
        [-1, 1, 0],
        [-1, -1, 0],
        [-1, 0, 1],
        [-1, 0, -1],
        [0, 1, 0],
        [0, -1, 0],
        [0, 0, 1],
        [0, 0, -1],
        [0, 1, 1],
        [0, 1, -1],
        [0, -1, 1],
        [0, -1, -1],
    ]
)
tau_base = 0.6
smagorinsky = 0.17


def collide(h):
    def pair(first, second):
        return h[first] + h[second], h[first] - h[second]

    s_x, d_x = pair(1, 6)
    s_xyp, d_xyp = pair(2, 8)
    s_xym, d_xym = pair(3, 7)
    s_xzp, d_xzp = pair(4, 10)
    s_xzm, d_xzm = pair(5, 9)
    s_y, d_y = pair(11, 12)
    s_z, d_z = pair(13, 14)
    s_yzp, d_yzp = pair(15, 18)
    s_yzm, d_yzm = pair(16, 17)
    j_x = (d_x + d_x) + (d_xyp + d_xym) + (d_xzp + d_xzm)
    j_y = (d_y + d_y) + (d_xyp - d_xym) + (d_yzp + d_yzm)
    j_z = (d_z + d_z) + (d_xzp - d_xzm) + (d_yzp - d_yzm)
    t_xy, t_xz, t_yz = s_xyp + s_xym, s_xzp + s_xzm, s_yzp + s_yzm
    m_xy, m_xz, m_yz = s_xyp - s_xym, s_xzp - s_xzm, s_yzp - s_yzm
    ss_x, ss_y, ss_z = s_x + s_x, s_y + s_y, s_z + s_z
    yz_part = ss_y + t_yz
    m_xx = ss_x + (t_xy + t_xz)
    m_yy = yz_part + t_xy
    m_zz = ss_z + (t_xz + t_yz)
    rho36 = (12.0 * h[0] + ss_z) + (m_xx + yz_part)
    inverse = 1.0 / rho36
    k_u = 1.5 * inverse
    k_p = 2.25 * inverse
    u_x, u_y, u_z = j_x * k_u, j_y * k_u, j_z * k_u
    xx, yy, zz = u_x * u_x, u_y * u_y, u_z * u_z
    xy, xz, yz = u_x * u_y, u_x * u_z, u_y * u_z
    p_xx = m_xx * k_p - (xx + 0.75)
    p_yy = m_yy * k_p - (yy + 0.75)
    p_zz = m_zz * k_p - (zz + 0.75)
    p_xy = m_xy * k_p - xy
    p_xz = m_xz * k_p - xz
    p_yz = m_yz * k_p - yz
    off = p_xy * p_xy + p_xz * p_xz + p_yz * p_yz
    square = (p_xx * p_xx + p_yy * p_yy) + (p_zz * p_zz + (off + off))
    magnitude = square * lax.rsqrt(jnp.maximum(square, 1e-30))
    factor = 18.0 * np.sqrt(2.0) * smagorinsky * smagorinsky / 2.25
    inner = tau_base * tau_base + float(factor) * magnitude
    omega = 2.0 / (tau_base + inner * lax.rsqrt(inner))
    keep = 1.0 - omega
    gain = (omega * (1.0 / 36.0)) * rho36
    gain2 = gain + gain
    rest = gain - gain * ((2.0 / 3.0) * ((xx + yy) + zz))
    gain4 = gain2 + gain2
    a_x, a_y, a_z = gain2 * u_x, gain2 * u_y, gain2 * u_z
    b_x, b_y, b_z = a_x * u_x, a_y * u_y, a_z * u_z
    n_x, n_y, n_z = rest + b_x, rest + b_y, rest + b_z
    out = [None] * DIRS
    out[0] = keep * h[0] + rest

    def spread(first, second, even, odd):
        out[first] = keep * h[first] + (even + odd)
        out[second] = keep * h[second] + (even - odd)

    spread(1, 6, n_x, a_x)
    spread(11, 12, n_y, a_y)
    spread(13, 14, n_z, a_z)
    for plus, minus, base, cross, first, second in (
        ((2, 8), (3, 7), n_x + b_y, gain4 * xy, a_x, a_y),
        ((4, 10), (5, 9), n_x + b_z, gain4 * xz, a_x, a_z),
        ((15, 18), (16, 17), n_y + b_z, gain4 * yz, a_y, a_z),
    ):
        spread(*plus, base + cross, first + second)
        spread(*minus, base - cross, first - second)
    return out


def lane_sources(step_y, step_z):
    lane = lax.broadcasted_iota(jnp.int32, (8, LANES), 1)
    along_y = (lane - step_y * BZ) & (LANES - 1) & ~(BZ - 1)
    along_z = (lane - step_z) & (BZ - 1)
    return along_y | along_z


def moves():
    lane = lax.broadcasted_iota(jnp.int32, (8, LANES), 1)
    index = {}
    for step_y in (-1, 0, 1):
        for step_z in (-1, 1):
            index[step_y, step_z] = lane_sources(step_y, step_z)
    border = {1: lane < BZ, -1: lane >= LANES - BZ}
    return index, border


def shift_cross(lower, upper, direction, tables):
    index, border = tables
    step_y, step_z = int(VELOCITY[direction, 1]), int(VELOCITY[direction, 2])
    if step_z != 0:
        source = index[step_y, step_z]
        lower = jnp.take_along_axis(lower, source, axis=1, mode="promise_in_bounds")
        upper = jnp.take_along_axis(upper, source, axis=1, mode="promise_in_bounds")
    elif step_y != 0:
        lower = pltpu.roll(lower, (step_y * BZ) % LANES, 1)
        upper = pltpu.roll(upper, (step_y * BZ) % LANES, 1)
    if step_y != 0:
        edge = border[step_y]
        lower, upper = jnp.where(edge, upper, lower), jnp.where(edge, lower, upper)
    return lower, upper


def layout_of(sub_count, old_ref, new_ref, curve, sub):
    old_start, new_start = 0, 0
    for other in range(sub_count - 1):
        before = other < sub
        old_start += jnp.where(before, old_ref[other, curve], 0)
        new_start += jnp.where(before, new_ref[other, curve], 0)
    held_old = old_ref[sub, curve] * BX
    held_new = new_ref[sub, curve] * BX
    return held_old, held_new, (new_start - old_start) * BX


def pack_kernel(
    sub_count, old_hbm, new_hbm, pop_ref, one_ref, two_ref, all_ref, info_ref, old_ref, new_ref, sem,
):
    curve, sub = lax.axis_index("curve"), lax.axis_index("sub")
    counts = [
        pltpu.make_async_copy(source, target, sem.at[at])
        for at, (source, target) in enumerate(((old_hbm, old_ref), (new_hbm, new_ref)))
    ]
    loads = [
        pltpu.make_async_copy(
            pop_ref.at[:, :, half * LANES : (half + 1) * LANES], all_ref.at[:, half], sem.at[2 + half]
        )
        for half in range(HALVES)
    ]
    for load in counts + loads:
        load.start()
    for load in counts:
        load.wait()
    held_old, held_new, offset = layout_of(sub_count, old_ref, new_ref, curve, sub)
    info_ref[0] = held_old
    info_ref[1] = held_new
    info_ref[2] = offset
    for load in loads:
        load.wait()
    even = sub % 2 == 0
    right = held_old - SPLIT
    for target, start, count in (
        (one_ref, jnp.where(even, right, 0), SPLIT),
        (two_ref, jnp.where(even, 0, right), SPLIT),
    ):
        for direction in range(DIRS):
            for half in range(HALVES):
                row = (direction * HALVES + half) * count
                target[row : row + count, :] = all_ref[direction, half, pl.ds(start, count), :]


def both(first, second):
    return jnp.logical_and(first, second)


def fetch(source, row, moved):
    return [
        [source[direction, half, pl.ds(row - int(VELOCITY[direction, 0]) * moved, 8), :] for direction in range(DIRS)]
        for half in range(HALVES)
    ]


def shift(halves, tables):
    moved = [shift_cross(halves[0][direction], halves[1][direction], direction, tables) for direction in range(DIRS)]
    return [[pair[half] for pair in moved] for half in range(HALVES)]


def store(target, row, halves):
    for half in range(HALVES):
        for direction in range(DIRS):
            target[direction, half, pl.ds(row, 8), :] = halves[half][direction]


def rim_parts(side):
    parts, row = [], 0
    for half in range(HALVES):
        for directions, count in ((TOWARD[side], 4), (LEVEL, 3), (TOWARD[1 - side], 2)):
            for direction in directions:
                parts.append((direction, half, row, 0 if side == 0 else STEPS - count, count))
                row += count
    return parts


RIM = sum(part[-1] for part in rim_parts(0))


def rim_kernel(sub_count, info_ref, cells_ref, far_ref):
    sub = lax.axis_index("sub")
    tables = moves()

    def send(side, row):
        relaxed = shift([collide(half) for half in fetch(cells_ref, row, 0)], tables)
        for direction, half, at, first, count in rim_parts(side):
            first += STEPS * side
            far_ref[at : at + count, :] = relaxed[half][direction][first : first + count, :]

    @pl.when(sub == 0)
    def _():
        send(0, 0)

    @pl.when(sub == sub_count - 1)
    def _():
        send(1, pl.multiple_of(info_ref[0] - 8, 8))


REST = BX - SPLIT
RAW_ROWS = DIRS * HALVES * REST
MORE = RAW_ROWS + STEPS * 5 * HALVES


def ahead_kernel(sub_count, first, info_ref, cells_ref, *refs):
    one_ref, two_ref, ping_ref, pong_ref = refs if first else refs[2:]
    sub = lax.axis_index("sub")
    held_old = info_ref[0]
    even = sub % 2 == 0
    tables = moves()

    def side_parts(side):
        return (BX - 4, 4, SPLIT) if side == 0 else (held_old - BX - 4, 3, held_old - BX)

    def step_sides(jobs):
        for step in range(STEPS):
            source, target = (ping_ref, pong_ref) if step % 2 else (pong_ref, ping_ref)
            groups = []
            for side, _ in jobs:
                if step == 0:
                    groups.append(fetch(cells_ref, side_parts(side)[0], 0))
                else:
                    groups.append(fetch(source.at[side], PAD, 1))
            relaxed = [shift([collide(half) for half in halves], tables) for halves in groups]
            for (side, message), halves in zip(jobs, relaxed):
                if step < STEPS - 1:
                    store(target.at[side], PAD, halves)
                at = side_parts(side)[1]
                for half in range(HALVES):
                    for number, direction in enumerate(TOWARD[side]):
                        row = RAW_ROWS + (step * 5 + number) * HALVES + half
                        message[row : row + 1, :] = halves[half][direction][at : at + 1, :]
        for side, message in jobs:
            for direction in range(DIRS):
                for half in range(HALVES):
                    row = (direction * HALVES + half) * REST
                    message[row : row + REST, :] = cells_ref[direction, half, pl.ds(side_parts(side)[2], REST), :]

    if first:

        @pl.when(sub == 0)
        def _():
            step_sides([(1, one_ref)])

    else:

        @pl.when(sub == sub_count - 1)
        def _():
            step_sides([(0, one_ref)])

        middle = both(sub > 0, sub < sub_count - 1)

        @pl.when(both(middle, even))
        def _():
            step_sides([(1, one_ref), (0, two_ref)])

        @pl.when(both(middle, jnp.logical_not(even)))
        def _():
            step_sides([(0, one_ref), (1, two_ref)])


def inner_kernel(
    slots, info_ref, first_ref, out_ref, own_ref, next_ref, cross_ref, edge_ref,
    ping_ref, pong_ref, raw_ref, tile_ref, zero_ref, out_sem,
):
    held_old, held_new, offset = info_ref[0], info_ref[1], info_ref[2]
    end = offset + held_new

    def clear(slot):
        return pltpu.make_async_copy(
            zero_ref, out_ref.at[:, slot * BX : (slot + 1) * BX, :], out_sem.at[slot]
        )

    @pl.when(held_new < slots * BX)
    def _():
        zero_ref[...] = jnp.zeros_like(zero_ref)

    for slot in range(slots):

        @pl.when(slot * BX >= held_new)
        def _():
            clear(slot).start()

    for direction in range(DIRS):
        for half in range(HALVES):
            own_ref[direction, half, :STEPS, :] = first_ref[direction, half, :STEPS, :]
            own_ref[direction, half, STEPS:, :] = first_ref[direction, half, pl.ds(held_old - STEPS, STEPS), :]
    tables = moves()
    last = held_old - STEPS - 1 + PAD
    pairs = held_old // 16

    def run(step, source, target):
        def settle(row):
            waiting = [fetch(raw_ref, at, 0) for at in (0, 8)]
            return [shift(halves, tables) for halves in waiting], (row, row + 8)

        def body(pair, carry):
            row = pl.multiple_of(pair * 16, 16)
            top = row if step == 0 else row + PAD
            values, rows = settle(pl.multiple_of(PAD + 16 * jnp.maximum(pair - 1, 0), 8))
            cells = [fetch(source, at, 1 if step else 0) for at in (top, top + 8)]
            relaxed = [[collide(half) for half in halves] for halves in cells]
            for at, halves in zip(rows, values):
                store(target, at, halves)
            for at, halves in zip((0, 8), relaxed):
                store(raw_ref, at, halves)
            return carry

        lax.fori_loop(0, pairs, body, 0)
        values, rows = settle(pl.multiple_of(PAD + 16 * (pairs - 1), 8))
        for at, halves in zip(rows, values):
            store(target, at, halves)
        for side, first in ((0, 6), (1, 1)):
            for at in range(5):
                for half in range(HALVES):
                    row = last if side else PAD + STEPS
                    cross_ref[((step * 2 + side) * 5 + at) * HALVES + half, :] = target[
                        first + at, half, row, :
                    ]

    run(0, first_ref, ping_ref)
    for direction in range(DIRS):
        for half in range(HALVES):
            next_ref[direction, half, :STEPS, :] = ping_ref[direction, half, PAD : PAD + STEPS, :]
            next_ref[direction, half, STEPS:, :] = ping_ref[direction, half, pl.ds(last + 1, STEPS), :]
    run(1, ping_ref, pong_ref)
    run(2, pong_ref, ping_ref)
    run(3, ping_ref, pong_ref)

    tiles = slots * BX // 8

    def write(tile):
        row = pl.multiple_of(jnp.clip(tile * 8 - offset, 0, (tiles - 1) * 8), 8)
        return pltpu.make_async_copy(
            tile_ref.at[:, tile * 8 : tile * 8 + 8, :], out_ref.at[:, pl.ds(row, 8), :], out_sem.at[slots + tile]
        )

    def kept(tile):
        inside = jnp.logical_and(tile * 8 >= offset, tile * 8 < end)
        return jnp.logical_and(inside, tile * 8 < held_old - 8)

    for tile in range(tiles):

        @pl.when(tile * 8 < held_old)
        def _():
            halves = fetch(pong_ref, PAD + tile * 8, 1)
            for direction in range(DIRS):
                for half in range(HALVES):
                    lanes = slice(half * LANES, (half + 1) * LANES)
                    tile_ref[direction, tile * 8 : tile * 8 + 8, lanes] = halves[half][direction]

        if tile > 0:

            @pl.when(kept(tile))
            def _():
                write(tile).start()

    right = pl.multiple_of(held_old - 8, 8)
    for direction in range(DIRS):
        edge_ref[direction, 0:8, :] = tile_ref[direction, 0:8, :]
        edge_ref[direction, 8:16, :] = tile_ref[direction, pl.ds(right, 8), :]
    for slot in range(slots):

        @pl.when(slot * BX >= held_new)
        def _():
            clear(slot).wait()

    for tile in range(1, tiles):

        @pl.when(kept(tile))
        def _():
            write(tile).wait()


def finish(side, source, merged, whole, row, edge_ref, out_ref, done_ref, sem):
    plane = lax.broadcasted_iota(jnp.int32, (8, LANES), 0)
    mine = plane < STEPS if side == 0 else plane >= STEPS
    for at, start in [merged] + whole:
        halves = fetch(source, start, 1)
        for direction in range(DIRS):
            for half in range(HALVES):
                lanes = slice(half * LANES, (half + 1) * LANES)
                value = halves[half][direction]
                if (at, start) == merged:
                    value = jnp.where(mine, value, edge_ref[direction, side * 8 : side * 8 + 8, lanes])
                done_ref[direction, at : at + 8, lanes] = value
    low, count = min(at for at, _ in [merged] + whole), 8 + 8 * len(whole)
    copy = pltpu.make_async_copy(
        done_ref.at[:, low : low + count, :], out_ref.at[:, pl.ds(pl.multiple_of(row, 8), count), :], sem
    )
    copy.start()
    return copy


def tail_kernel(
    sub_count, info_ref, own_ref, next_ref, cross_ref, edge_ref, one_ref, also_ref, more_ref, two_ref, last_ref,
    far_ref, _, out_ref, left_ref, right_ref, raw_ref, left_done_ref, right_done_ref, sem,
):
    sub = lax.axis_index("sub")
    held_old, held_new, offset = info_ref[0], info_ref[1], info_ref[2]
    gained = offset + held_new - held_old
    lefts = jnp.where(offset == 0, 1, jnp.where(offset < 0, 3, 0))
    rights = jnp.where(gained == 0, 1, jnp.where(gained > 0, 3, 0))
    outer_left, outer_right = sub == 0, sub == sub_count - 1
    inner_left, inner_right = jnp.logical_not(outer_left), jnp.logical_not(outer_right)
    even = sub % 2 == 0
    odd = jnp.logical_not(even)
    later = sub // 2 % 2 == 1
    sooner = jnp.logical_not(later)

    def place(target, source, count, first, used, start):
        for direction in range(DIRS):
            for half in range(HALVES):
                row = (direction * HALVES + half) * count + first
                target[0, direction, half, start : start + used, :] = source[row : row + used, :]

    def near_part(side, target, source, here, count):
        @pl.when(both(here, count == 3))
        def _():
            place(target, source, SPLIT, 0, SPLIT, EDGE - SPLIT if side == 0 else BX)

        @pl.when(both(here, count == 1))
        def _():
            place(target, source, SPLIT, SPLIT - STEPS if side == 0 else 0, STEPS, EDGE - STEPS if side == 0 else BX)

    def more_part(side, target, source, here, count):
        @pl.when(both(here, count == 3))
        def _():
            place(target, source, REST, 0, REST, PAD if side == 0 else BX + SPLIT)
            border = PAD - 1 if side == 0 else 2 * BX
            for step in range(STEPS):
                for number, direction in enumerate(TOWARD[1 - side]):
                    for half in range(HALVES):
                        row = RAW_ROWS + (step * 5 + number) * HALVES + half
                        target[step + 1, direction, half, border, :] = source[row, :]

    near_part(0, left_ref, one_ref, both(odd, sooner), lefts)
    near_part(0, left_ref, also_ref, both(odd, later), lefts)
    near_part(1, right_ref, one_ref, both(even, sooner), rights)
    near_part(1, right_ref, also_ref, both(even, later), rights)
    near_part(0, left_ref, two_ref, both(even, inner_left), lefts)
    near_part(1, right_ref, two_ref, both(odd, inner_right), rights)
    more_part(0, left_ref, more_ref, odd, lefts)
    more_part(1, right_ref, more_ref, even, rights)
    more_part(0, left_ref, last_ref, both(even, inner_left), lefts)
    more_part(1, right_ref, last_ref, both(odd, inner_right), rights)

    for side, target, here in ((0, left_ref, outer_left), (1, right_ref, outer_right)):

        @pl.when(here)
        def _():
            beside, own = (EDGE - STEPS, EDGE) if side == 0 else (BX, BX - STEPS)
            for direction, half, at, first, count in rim_parts(1 - side):
                target[1, direction, half, beside + first : beside + first + count, :] = far_ref[at : at + count, :]
            for direction in range(DIRS):
                for half in range(HALVES):
                    target[1, direction, half, own : own + STEPS, :] = next_ref[
                        direction, half, side * STEPS : (side + 1) * STEPS, :
                    ]

    for side, target, count, start, border in (
        (0, left_ref, lefts, EDGE, EDGE + STEPS),
        (1, right_ref, rights, BX - STEPS, BX - STEPS - 1),
    ):

        @pl.when(count > 0)
        def _():
            for direction in range(DIRS):
                for half in range(HALVES):
                    target[0, direction, half, start : start + STEPS, :] = own_ref[
                        direction, half, side * STEPS : (side + 1) * STEPS, :
                    ]
            for step in range(STEPS):
                for at in range(5):
                    for half in range(HALVES):
                        target[step + 1, TOWARD[side][at], half, border, :] = cross_ref[
                            ((step * 2 + side) * 5 + at) * HALVES + half, :
                        ]

    tables = moves()
    skips = [jnp.where(here, 1, 0) for here in (outer_left, outer_right)]

    def groups_of(side, count):
        if count == 1:
            return [(EDGE - STEPS if side == 0 else BX - STEPS, 0, 8)]
        if side == 0:
            return [(PAD, 0, 8), (PAD + 8, 0, 8), (EDGE, 0, STEPS)]
        return [(PAD, STEPS, STEPS), (BX, 0, 8), (BX + 8, 0, 8)]

    strips = (left_ref, right_ref)

    def put(target, group, halves):
        row, low, count = group
        for half in range(HALVES):
            for direction in range(DIRS):
                value = halves[half][direction]
                target[direction, half, row + low : row + low + count, :] = value[low : low + count, :]

    def plain(side, count, start):
        groups, strip = groups_of(side, count), strips[side]

        def body(step, carry):
            cells = [fetch(strip.at[step], group[0], jnp.minimum(step, 1)) for group in groups]
            relaxed = [shift([collide(half) for half in halves], tables) for halves in cells]
            for group, halves in zip(groups, relaxed):
                put(strip.at[step + 1], group, halves)
            return carry

        lax.fori_loop(start, STEPS, body, 0)

    def staggered(first, first_count, second_count):
        one, two = strips[first], strips[1 - first]
        first_groups, second_groups = groups_of(first, first_count), groups_of(1 - first, second_count)

        def settle(into):
            for at, group in enumerate(second_groups):
                put(two.at[into], group, shift(fetch(raw_ref, 8 * at, 0), tables))

        def body(step, carry):
            moved = jnp.minimum(step, 1)
            settle(jnp.where(step <= skips[1 - first], STEPS + 1, step))
            into = jnp.where(step < skips[first], STEPS + 1, step + 1)
            cells = [fetch(one.at[step], group[0], moved) for group in first_groups]
            relaxed = [[collide(half) for half in halves] for halves in cells]
            for group, halves in zip(first_groups, relaxed):
                put(one.at[into], group, shift(halves, tables))
            cells = [fetch(two.at[step], group[0], moved) for group in second_groups]
            relaxed = [[collide(half) for half in halves] for halves in cells]
            for at, halves in enumerate(relaxed):
                store(raw_ref, 8 * at, halves)
            return carry

        lax.fori_loop(0, STEPS, body, 0)
        settle(STEPS)

    for first, counts in ((0, (1, 1)), (0, (3, 1)), (1, (1, 3)), (0, (3, 3))):

        @pl.when(both(lefts == counts[0], rights == counts[1]))
        def _():
            staggered(first, counts[first], counts[1 - first])

    for count in (1, 3):

        @pl.when(both(lefts == count, rights == 0))
        def _():
            plain(0, count, skips[0])

        @pl.when(both(lefts == 0, rights == count))
        def _():
            plain(1, count, skips[1])

    row = held_old - 8 - offset
    ends = (
        (lefts, 0, left_ref, (16, EDGE), [(0, PAD), (8, PAD + 8)], 0, left_done_ref),
        (rights, 1, right_ref, (0, PAD), [(8, BX), (16, BX + 8)], row, right_done_ref),
    )
    for count, side, source, merged, whole, to, done in ends:
        for amount, used in ((3, whole), (1, [])):

            @pl.when(count == amount)
            def _():
                finish(side, source.at[STEPS], merged, used, to, edge_ref, out_ref, done, sem.at[side])

    for count, side, _, merged, whole, to, done in ends:
        for amount in (3, 1):

            @pl.when(count == amount)
            def _():
                size = 8 * amount
                start = 0 if amount == 3 else merged[0]
                pltpu.make_async_copy(
                    done.at[:, start : start + size, :],
                    out_ref.at[:, pl.ds(pl.multiple_of(to, 8), size), :],
                    sem.at[side],
                ).wait()


def shards(populations, count_old, count_new):
    curve_count, sub_count = lax.axis_size("curve"), lax.axis_size("sub")
    planes = populations.shape[1]
    slots = planes // BX
    total = curve_count * sub_count
    old, new = count_old.T, count_new.T
    smem = pl.BlockSpec(memory_space=pltpu.SMEM)
    hbm = pl.BlockSpec(memory_space=pltpu.HBM)
    vmem = pl.BlockSpec(memory_space=pltpu.VMEM)
    rows = DIRS * HALVES
    whole = jax.ShapeDtypeStruct(populations.shape, jnp.float32)

    def local(*shape):
        return pltpu.VMEM(shape, jnp.float32)

    def near(value):
        return pltpu.with_memory_space_constraint(value, pltpu.VMEM)

    params = pltpu.CompilerParams(vmem_limit_bytes=32 << 20)
    populations, old, new = (
        pltpu.with_memory_space_constraint(value, pltpu.HBM) for value in (populations, old, new)
    )
    one, two, cells, info = pl.pallas_call(
        functools.partial(pack_kernel, sub_count),
        out_shape=(
            local(rows * SPLIT, LANES),
            local(rows * SPLIT, LANES),
            local(DIRS, HALVES, planes, LANES),
            pltpu.SMEM((4,), jnp.int32),
        ),
        in_specs=[hbm, hbm, hbm],
        out_specs=(vmem, vmem, vmem, smem),
        scratch_shapes=[
            pltpu.SMEM(old.shape, jnp.int32),
            pltpu.SMEM(old.shape, jnp.int32),
            pltpu.SemaphoreType.DMA((2 + HALVES,)),
        ],
        compiler_params=params,
        name="pack",
    )(old, new, populations)
    info = pltpu.with_memory_space_constraint(info, pltpu.SMEM)
    cells = near(cells)
    axes = ("curve", "sub")

    def everyone(pairs):
        busy = {source for source, _ in pairs}
        rest = [at for at in range(total) if at not in busy]
        return pairs + [(at, (at // sub_count ^ 1) * sub_count + at % sub_count) for at in rest]

    def send(value, pairs):
        return lax.ppermute(value, axes, pairs)

    inside = [(at, at ^ 1) for at in range(total)]
    between, across = [], []
    for at in range(1, total, 2):
        after = (at + 1) % total
        into = across if after % sub_count == 0 else between
        into += [(at, after), (after, at)]
    sooner = [(at, beside) for at, beside in inside if at % sub_count // 2 % 2 == 0]
    later = [(at, beside) for at, beside in inside if at % sub_count // 2 % 2 == 1]
    ends = one
    one = send(ends, everyone(sooner))
    two = send(two, everyone(between))
    also = send(ends, everyone(later))
    rim = pl.pallas_call(
        functools.partial(rim_kernel, sub_count),
        out_shape=local(RIM, LANES),
        in_specs=[smem, vmem],
        out_specs=vmem,
        compiler_params=params,
        name="rim",
    )(info, cells)
    around = pltpu.VMEM((2, DIRS, HALVES, 3 * PAD, LANES), jnp.float32)
    more, last = pl.pallas_call(
        functools.partial(ahead_kernel, sub_count, True),
        out_shape=(local(MORE, LANES), local(MORE, LANES)),
        in_specs=[smem, vmem],
        out_specs=(vmem, vmem),
        scratch_shapes=[around, around],
        compiler_params=params,
        cost_estimate=pl.CostEstimate(flops=10**6, bytes_accessed=10**5, transcendentals=0),
        name="ahead_first",
    )(info, cells)
    first_done = more
    rim = send(lax.optimization_barrier((rim, first_done))[0], everyone(across))
    more, last = pl.pallas_call(
        functools.partial(ahead_kernel, sub_count, False),
        out_shape=(local(MORE, LANES), local(MORE, LANES)),
        in_specs=[smem, vmem, vmem, vmem],
        out_specs=(vmem, vmem),
        scratch_shapes=[around, around],
        input_output_aliases={2: 0, 3: 1},
        compiler_params=params,
        cost_estimate=pl.CostEstimate(flops=10**6, bytes_accessed=10**5, transcendentals=0),
        name="ahead",
    )(info, cells, near(more), near(last))
    last = send(last, everyone(between))
    more = send(more, inside)
    state = pltpu.VMEM((DIRS, HALVES, planes + 2 * PAD, LANES), jnp.float32)
    result, own, following, cross, edge = pl.pallas_call(
        functools.partial(inner_kernel, slots),
        out_shape=(
            whole,
            local(DIRS, HALVES, 2 * STEPS, LANES),
            local(DIRS, HALVES, 2 * STEPS, LANES),
            local(STEPS * 2 * 5 * HALVES, LANES),
            local(DIRS, 16, HALVES * LANES),
        ),
        in_specs=[smem, vmem],
        out_specs=(hbm, vmem, vmem, vmem, vmem),
        scratch_shapes=[
            state,
            state,
            pltpu.VMEM((DIRS, HALVES, 16, LANES), jnp.float32),
            pltpu.VMEM(populations.shape, jnp.float32),
            pltpu.VMEM((DIRS, BX, HALVES * LANES), jnp.float32),
            pltpu.SemaphoreType.DMA((slots + slots * BX // 8,)),
        ],
        compiler_params=params,
        cost_estimate=pl.CostEstimate(flops=10**9, bytes_accessed=8 * 10**6, transcendentals=0),
        name="inner",
    )(info, cells)
    own, following, cross, edge = map(near, (own, following, cross, edge))
    return pl.pallas_call(
        functools.partial(tail_kernel, sub_count),
        out_shape=whole,
        in_specs=[smem] + [vmem] * 10 + [hbm],
        out_specs=hbm,
        scratch_shapes=[
            pltpu.VMEM((STEPS + 2, DIRS, HALVES, STRIP, LANES), jnp.float32),
            pltpu.VMEM((STEPS + 2, DIRS, HALVES, STRIP, LANES), jnp.float32),
            pltpu.VMEM((DIRS, HALVES, 24, LANES), jnp.float32),
            pltpu.VMEM((DIRS, 24, HALVES * LANES), jnp.float32),
            pltpu.VMEM((DIRS, 24, HALVES * LANES), jnp.float32),
            pltpu.SemaphoreType.DMA((2,)),
        ],
        input_output_aliases={11: 0},
        compiler_params=params,
        cost_estimate=pl.CostEstimate(flops=10**8, bytes_accessed=10**6, transcendentals=0),
        name="tail",
    )(info, own, following, cross, edge, *map(near, (one, also, more, two, last, rim)), result)


def solution(mesh):
    if mesh.shape["sub"] % 2 or mesh.shape["curve"] % 2:
        raise ValueError("odd mesh")
    in_specs = (P(None, ("curve", "sub"), None), P(), P())
    out_specs = P(None, ("curve", "sub"), None)
    return jax.shard_map(shards, mesh=mesh, in_specs=in_specs, out_specs=out_specs, check_vma=False)
```

```python
import functools

import jax
import jax.numpy as jnp
import numpy as np
from jax import lax
from jax.experimental import pallas as pl
from jax.experimental.pallas import tpu as pltpu
from jax.sharding import PartitionSpec as P

BX = 16
BZ = 16
STEPS = 4
DIRS = 19
LANES = 128
HALVES = 2
PAD = 8
STRIP = 40
EDGE = 24
SPLIT = 11
SPLIT_TWO = 15
TOWARD = {0: (6, 7, 8, 9, 10), 1: (1, 2, 3, 4, 5)}
LEVEL = (0, 11, 12, 13, 14, 15, 16, 17, 18)

VELOCITY = np.array(
    [
        [0, 0, 0],
        [1, 0, 0],
        [1, 1, 0],
        [1, -1, 0],
        [1, 0, 1],
        [1, 0, -1],
        [-1, 0, 0],
        [-1, 1, 0],
        [-1, -1, 0],
        [-1, 0, 1],
        [-1, 0, -1],
        [0, 1, 0],
        [0, -1, 0],
        [0, 0, 1],
        [0, 0, -1],
        [0, 1, 1],
        [0, 1, -1],
        [0, -1, 1],
        [0, -1, -1],
    ]
)
tau_base = 0.6
smagorinsky = 0.17


def collide(h):
    def pair(first, second):
        return h[first] + h[second], h[first] - h[second]

    s_x, d_x = pair(1, 6)
    s_xyp, d_xyp = pair(2, 8)
    s_xym, d_xym = pair(3, 7)
    s_xzp, d_xzp = pair(4, 10)
    s_xzm, d_xzm = pair(5, 9)
    s_y, d_y = pair(11, 12)
    s_z, d_z = pair(13, 14)
    s_yzp, d_yzp = pair(15, 18)
    s_yzm, d_yzm = pair(16, 17)
    j_x = (d_x + d_x) + (d_xyp + d_xym) + (d_xzp + d_xzm)
    j_y = (d_y + d_y) + (d_xyp - d_xym) + (d_yzp + d_yzm)
    j_z = (d_z + d_z) + (d_xzp - d_xzm) + (d_yzp - d_yzm)
    t_xy, t_xz, t_yz = s_xyp + s_xym, s_xzp + s_xzm, s_yzp + s_yzm
    m_xy, m_xz, m_yz = s_xyp - s_xym, s_xzp - s_xzm, s_yzp - s_yzm
    ss_x, ss_y, ss_z = s_x + s_x, s_y + s_y, s_z + s_z
    yz_part = ss_y + t_yz
    m_xx = ss_x + (t_xy + t_xz)
    m_yy = yz_part + t_xy
    m_zz = ss_z + (t_xz + t_yz)
    rho36 = (12.0 * h[0] + ss_z) + (m_xx + yz_part)
    inverse = 1.0 / rho36
    k_u = 1.5 * inverse
    k_p = 2.25 * inverse
    u_x, u_y, u_z = j_x * k_u, j_y * k_u, j_z * k_u
    xx, yy, zz = u_x * u_x, u_y * u_y, u_z * u_z
    xy, xz, yz = u_x * u_y, u_x * u_z, u_y * u_z
    p_xx = m_xx * k_p - (xx + 0.75)
    p_yy = m_yy * k_p - (yy + 0.75)
    p_zz = m_zz * k_p - (zz + 0.75)
    p_xy = m_xy * k_p - xy
    p_xz = m_xz * k_p - xz
    p_yz = m_yz * k_p - yz
    off = p_xy * p_xy + p_xz * p_xz + p_yz * p_yz
    square = (p_xx * p_xx + p_yy * p_yy) + (p_zz * p_zz + (off + off))
    magnitude = square * lax.rsqrt(jnp.maximum(square, 1e-30))
    factor = 18.0 * np.sqrt(2.0) * smagorinsky * smagorinsky / 2.25
    inner = tau_base * tau_base + float(factor) * magnitude
    omega = 2.0 / (tau_base + inner * lax.rsqrt(inner))
    keep = 1.0 - omega
    gain = (omega * (1.0 / 36.0)) * rho36
    gain2 = gain + gain
    rest = gain - gain * ((2.0 / 3.0) * ((xx + yy) + zz))
    gain4 = gain2 + gain2
    a_x, a_y, a_z = gain2 * u_x, gain2 * u_y, gain2 * u_z
    b_x, b_y, b_z = a_x * u_x, a_y * u_y, a_z * u_z
    n_x, n_y, n_z = rest + b_x, rest + b_y, rest + b_z
    out = [None] * DIRS
    out[0] = keep * h[0] + rest

    def spread(first, second, even, odd):
        out[first] = keep * h[first] + (even + odd)
        out[second] = keep * h[second] + (even - odd)

    spread(1, 6, n_x, a_x)
    spread(11, 12, n_y, a_y)
    spread(13, 14, n_z, a_z)
    for plus, minus, base, cross, first, second in (
        ((2, 8), (3, 7), n_x + b_y, gain4 * xy, a_x, a_y),
        ((4, 10), (5, 9), n_x + b_z, gain4 * xz, a_x, a_z),
        ((15, 18), (16, 17), n_y + b_z, gain4 * yz, a_y, a_z),
    ):
        spread(*plus, base + cross, first + second)
        spread(*minus, base - cross, first - second)
    return out


def lane_sources(step_y, step_z):
    lane = lax.broadcasted_iota(jnp.int32, (8, LANES), 1)
    along_y = (lane - step_y * BZ) & (LANES - 1) & ~(BZ - 1)
    along_z = (lane - step_z) & (BZ - 1)
    return along_y | along_z


def moves():
    lane = lax.broadcasted_iota(jnp.int32, (8, LANES), 1)
    index = {}
    for step_y in (-1, 0, 1):
        for step_z in (-1, 1):
            index[step_y, step_z] = lane_sources(step_y, step_z)
    border = {1: lane < BZ, -1: lane >= LANES - BZ}
    return index, border


def shift_cross(lower, upper, direction, tables):
    index, border = tables
    step_y, step_z = int(VELOCITY[direction, 1]), int(VELOCITY[direction, 2])
    if step_z != 0:
        source = index[step_y, step_z]
        lower = jnp.take_along_axis(lower, source, axis=1, mode="promise_in_bounds")
        upper = jnp.take_along_axis(upper, source, axis=1, mode="promise_in_bounds")
    elif step_y != 0:
        lower = pltpu.roll(lower, (step_y * BZ) % LANES, 1)
        upper = pltpu.roll(upper, (step_y * BZ) % LANES, 1)
    if step_y != 0:
        edge = border[step_y]
        lower, upper = jnp.where(edge, upper, lower), jnp.where(edge, lower, upper)
    return lower, upper


def layout_of(sub_count, old_ref, new_ref, curve, sub):
    old_start, new_start = 0, 0
    for other in range(sub_count - 1):
        before = other < sub
        old_start += jnp.where(before, old_ref[other, curve], 0)
        new_start += jnp.where(before, new_ref[other, curve], 0)
    held_old = old_ref[sub, curve] * BX
    held_new = new_ref[sub, curve] * BX
    return held_old, held_new, (new_start - old_start) * BX


def pack_kernel(
    sub_count, old_hbm, new_hbm, pop_ref, one_ref, two_ref, all_ref, info_ref, old_ref, new_ref, sem,
):
    curve, sub = lax.axis_index("curve"), lax.axis_index("sub")
    counts = [
        pltpu.make_async_copy(source, target, sem.at[at])
        for at, (source, target) in enumerate(((old_hbm, old_ref), (new_hbm, new_ref)))
    ]
    loads = [
        pltpu.make_async_copy(
            pop_ref.at[:, :, half * LANES : (half + 1) * LANES], all_ref.at[:, half], sem.at[2 + half]
        )
        for half in range(HALVES)
    ]
    for load in counts + loads:
        load.start()
    for load in counts:
        load.wait()
    held_old, held_new, offset = layout_of(sub_count, old_ref, new_ref, curve, sub)
    info_ref[0] = held_old
    info_ref[1] = held_new
    info_ref[2] = offset
    for load in loads:
        load.wait()
    even = sub % 2 == 0
    for target, start, count in (
        (one_ref, jnp.where(even, held_old - SPLIT, 0), SPLIT),
        (two_ref, jnp.where(even, 0, held_old - SPLIT_TWO), SPLIT_TWO),
    ):
        for direction in range(DIRS):
            for half in range(HALVES):
                row = (direction * HALVES + half) * count
                target[row : row + count, :] = all_ref[direction, half, pl.ds(start, count), :]


def both(first, second):
    return jnp.logical_and(first, second)


def fetch(source, row, moved):
    return [
        [source[direction, half, pl.ds(row - int(VELOCITY[direction, 0]) * moved, 8), :] for direction in range(DIRS)]
        for half in range(HALVES)
    ]


def shift(halves, tables):
    moved = [shift_cross(halves[0][direction], halves[1][direction], direction, tables) for direction in range(DIRS)]
    return [[pair[half] for pair in moved] for half in range(HALVES)]


def store(target, row, halves):
    for half in range(HALVES):
        for direction in range(DIRS):
            target[direction, half, pl.ds(row, 8), :] = halves[half][direction]


def rim_parts(side):
    parts, row = [], 0
    for half in range(HALVES):
        for directions, count in ((TOWARD[side], 4), (LEVEL, 3), (TOWARD[1 - side], 2)):
            for direction in directions:
                parts.append((direction, half, row, 0 if side == 0 else STEPS - count, count))
                row += count
    return parts


RIM = sum(part[-1] for part in rim_parts(0))


def rim_kernel(sub_count, info_ref, cells_ref, far_ref):
    sub = lax.axis_index("sub")
    tables = moves()

    def send(side, row):
        relaxed = shift([collide(half) for half in fetch(cells_ref, row, 0)], tables)
        for direction, half, at, first, count in rim_parts(side):
            first += STEPS * side
            far_ref[at : at + count, :] = relaxed[half][direction][first : first + count, :]

    @pl.when(sub == 0)
    def _():
        send(0, 0)

    @pl.when(sub == sub_count - 1)
    def _():
        send(1, pl.multiple_of(info_ref[0] - 8, 8))


def raw_rows(split):
    return DIRS * HALVES * (BX - split)


def more_rows(split):
    return raw_rows(split) + STEPS * 5 * HALVES


def ahead_kernel(sub_count, first, info_ref, cells_ref, *refs):
    one_ref, two_ref, ping_ref, pong_ref = refs if first else refs[2:]
    sub = lax.axis_index("sub")
    held_old = info_ref[0]
    even = sub % 2 == 0
    tables = moves()

    def side_parts(side):
        return (BX - 4, 4) if side == 0 else (held_old - BX - 4, 3)

    def step_sides(jobs):
        for step in range(STEPS):
            source, target = (ping_ref, pong_ref) if step % 2 else (pong_ref, ping_ref)
            groups = []
            for side, _, _ in jobs:
                if step == 0:
                    groups.append(fetch(cells_ref, side_parts(side)[0], 0))
                else:
                    groups.append(fetch(source.at[side], PAD, 1))
            relaxed = [shift([collide(half) for half in halves], tables) for halves in groups]
            for (side, message, split), halves in zip(jobs, relaxed):
                if step < STEPS - 1:
                    store(target.at[side], PAD, halves)
                at = side_parts(side)[1]
                for half in range(HALVES):
                    for number, direction in enumerate(TOWARD[side]):
                        row = raw_rows(split) + (step * 5 + number) * HALVES + half
                        message[row : row + 1, :] = halves[half][direction][at : at + 1, :]
        for side, message, split in jobs:
            rest, start = BX - split, split if side == 0 else held_old - BX
            for direction in range(DIRS):
                for half in range(HALVES):
                    row = (direction * HALVES + half) * rest
                    message[row : row + rest, :] = cells_ref[direction, half, pl.ds(start, rest), :]

    if first:

        @pl.when(sub == 0)
        def _():
            step_sides([(1, one_ref, SPLIT)])

    else:

        @pl.when(sub == sub_count - 1)
        def _():
            step_sides([(0, one_ref, SPLIT)])

        middle = both(sub > 0, sub < sub_count - 1)

        @pl.when(both(middle, even))
        def _():
            step_sides([(1, one_ref, SPLIT), (0, two_ref, SPLIT_TWO)])

        @pl.when(both(middle, jnp.logical_not(even)))
        def _():
            step_sides([(0, one_ref, SPLIT), (1, two_ref, SPLIT_TWO)])


def inner_kernel(
    slots, info_ref, first_ref, out_ref, own_ref, next_ref, cross_ref, edge_ref,
    ping_ref, pong_ref, raw_ref, tile_ref, zero_ref, out_sem,
):
    held_old, held_new, offset = info_ref[0], info_ref[1], info_ref[2]
    end = offset + held_new

    def clear(slot):
        return pltpu.make_async_copy(
            zero_ref, out_ref.at[:, slot * BX : (slot + 1) * BX, :], out_sem.at[slot]
        )

    @pl.when(held_new < slots * BX)
    def _():
        zero_ref[...] = jnp.zeros_like(zero_ref)

    for slot in range(slots):

        @pl.when(slot * BX >= held_new)
        def _():
            clear(slot).start()

    for direction in range(DIRS):
        for half in range(HALVES):
            own_ref[direction, half, :STEPS, :] = first_ref[direction, half, :STEPS, :]
            own_ref[direction, half, STEPS:, :] = first_ref[direction, half, pl.ds(held_old - STEPS, STEPS), :]
    tables = moves()
    last = held_old - STEPS - 1 + PAD
    pairs = held_old // 16

    def run(step, source, target):
        def settle(row):
            waiting = [fetch(raw_ref, at, 0) for at in (0, 8)]
            return [shift(halves, tables) for halves in waiting], (row, row + 8)

        def body(pair, carry):
            row = pl.multiple_of(pair * 16, 16)
            top = row if step == 0 else row + PAD
            values, rows = settle(pl.multiple_of(PAD + 16 * jnp.maximum(pair - 1, 0), 8))
            cells = [fetch(source, at, 1 if step else 0) for at in (top, top + 8)]
            relaxed = [[collide(half) for half in halves] for halves in cells]
            for at, halves in zip(rows, values):
                store(target, at, halves)
            for at, halves in zip((0, 8), relaxed):
                store(raw_ref, at, halves)
            return carry

        lax.fori_loop(0, pairs, body, 0)
        values, rows = settle(pl.multiple_of(PAD + 16 * (pairs - 1), 8))
        for at, halves in zip(rows, values):
            store(target, at, halves)
        for side, first in ((0, 6), (1, 1)):
            for at in range(5):
                for half in range(HALVES):
                    row = last if side else PAD + STEPS
                    cross_ref[((step * 2 + side) * 5 + at) * HALVES + half, :] = target[
                        first + at, half, row, :
                    ]

    run(0, first_ref, ping_ref)
    for direction in range(DIRS):
        for half in range(HALVES):
            next_ref[direction, half, :STEPS, :] = ping_ref[direction, half, PAD : PAD + STEPS, :]
            next_ref[direction, half, STEPS:, :] = ping_ref[direction, half, pl.ds(last + 1, STEPS), :]
    run(1, ping_ref, pong_ref)
    run(2, pong_ref, ping_ref)
    run(3, ping_ref, pong_ref)

    tiles = slots * BX // 8

    def write(tile):
        row = pl.multiple_of(jnp.clip(tile * 8 - offset, 0, (tiles - 1) * 8), 8)
        return pltpu.make_async_copy(
            tile_ref.at[:, tile * 8 : tile * 8 + 8, :], out_ref.at[:, pl.ds(row, 8), :], out_sem.at[slots + tile]
        )

    def kept(tile):
        inside = jnp.logical_and(tile * 8 >= offset, tile * 8 < end)
        return jnp.logical_and(inside, tile * 8 < held_old - 8)

    for tile in range(tiles):

        @pl.when(tile * 8 < held_old)
        def _():
            halves = fetch(pong_ref, PAD + tile * 8, 1)
            for direction in range(DIRS):
                for half in range(HALVES):
                    lanes = slice(half * LANES, (half + 1) * LANES)
                    tile_ref[direction, tile * 8 : tile * 8 + 8, lanes] = halves[half][direction]

        if tile > 0:

            @pl.when(kept(tile))
            def _():
                write(tile).start()

    right = pl.multiple_of(held_old - 8, 8)
    for direction in range(DIRS):
        edge_ref[direction, 0:8, :] = tile_ref[direction, 0:8, :]
        edge_ref[direction, 8:16, :] = tile_ref[direction, pl.ds(right, 8), :]
    for slot in range(slots):

        @pl.when(slot * BX >= held_new)
        def _():
            clear(slot).wait()

    for tile in range(1, tiles):

        @pl.when(kept(tile))
        def _():
            write(tile).wait()


def finish(side, source, merged, whole, row, edge_ref, out_ref, done_ref, sem):
    plane = lax.broadcasted_iota(jnp.int32, (8, LANES), 0)
    mine = plane < STEPS if side == 0 else plane >= STEPS
    for at, start in [merged] + whole:
        halves = fetch(source, start, 1)
        for direction in range(DIRS):
            for half in range(HALVES):
                lanes = slice(half * LANES, (half + 1) * LANES)
                value = halves[half][direction]
                if (at, start) == merged:
                    value = jnp.where(mine, value, edge_ref[direction, side * 8 : side * 8 + 8, lanes])
                done_ref[direction, at : at + 8, lanes] = value
    low, count = min(at for at, _ in [merged] + whole), 8 + 8 * len(whole)
    copy = pltpu.make_async_copy(
        done_ref.at[:, low : low + count, :], out_ref.at[:, pl.ds(pl.multiple_of(row, 8), count), :], sem
    )
    copy.start()
    return copy


def tail_kernel(
    sub_count, info_ref, own_ref, next_ref, cross_ref, edge_ref, one_ref, also_ref, more_ref, two_ref, last_ref,
    far_ref, _, out_ref, left_ref, right_ref, raw_ref, left_done_ref, right_done_ref, sem,
):
    sub = lax.axis_index("sub")
    held_old, held_new, offset = info_ref[0], info_ref[1], info_ref[2]
    gained = offset + held_new - held_old
    lefts = jnp.where(offset == 0, 1, jnp.where(offset < 0, 3, 0))
    rights = jnp.where(gained == 0, 1, jnp.where(gained > 0, 3, 0))
    outer_left, outer_right = sub == 0, sub == sub_count - 1
    inner_left, inner_right = jnp.logical_not(outer_left), jnp.logical_not(outer_right)
    even = sub % 2 == 0
    odd = jnp.logical_not(even)
    later = sub // 2 % 2 == 1
    sooner = jnp.logical_not(later)

    def place(target, source, count, first, used, start):
        for direction in range(DIRS):
            for half in range(HALVES):
                row = (direction * HALVES + half) * count + first
                target[0, direction, half, start : start + used, :] = source[row : row + used, :]

    def near_part(side, target, source, here, count, split=SPLIT):
        @pl.when(both(here, count == 3))
        def _():
            place(target, source, split, 0, split, EDGE - split if side == 0 else BX)

        @pl.when(both(here, count == 1))
        def _():
            place(target, source, split, split - STEPS if side == 0 else 0, STEPS, EDGE - STEPS if side == 0 else BX)

    def more_part(side, target, source, here, count, split=SPLIT):
        @pl.when(both(here, count == 3))
        def _():
            place(target, source, BX - split, 0, BX - split, PAD if side == 0 else BX + split)
            border = PAD - 1 if side == 0 else 2 * BX
            for step in range(STEPS):
                for number, direction in enumerate(TOWARD[1 - side]):
                    for half in range(HALVES):
                        row = raw_rows(split) + (step * 5 + number) * HALVES + half
                        target[step + 1, direction, half, border, :] = source[row, :]

    near_part(0, left_ref, one_ref, both(odd, sooner), lefts)
    near_part(0, left_ref, also_ref, both(odd, later), lefts)
    near_part(1, right_ref, one_ref, both(even, sooner), rights)
    near_part(1, right_ref, also_ref, both(even, later), rights)
    near_part(0, left_ref, two_ref, both(even, inner_left), lefts, SPLIT_TWO)
    near_part(1, right_ref, two_ref, both(odd, inner_right), rights, SPLIT_TWO)
    more_part(0, left_ref, more_ref, odd, lefts)
    more_part(1, right_ref, more_ref, even, rights)
    more_part(0, left_ref, last_ref, both(even, inner_left), lefts, SPLIT_TWO)
    more_part(1, right_ref, last_ref, both(odd, inner_right), rights, SPLIT_TWO)

    for side, target, here in ((0, left_ref, outer_left), (1, right_ref, outer_right)):

        @pl.when(here)
        def _():
            beside, own = (EDGE - STEPS, EDGE) if side == 0 else (BX, BX - STEPS)
            for direction, half, at, first, count in rim_parts(1 - side):
                target[1, direction, half, beside + first : beside + first + count, :] = far_ref[at : at + count, :]
            for direction in range(DIRS):
                for half in range(HALVES):
                    target[1, direction, half, own : own + STEPS, :] = next_ref[
                        direction, half, side * STEPS : (side + 1) * STEPS, :
                    ]

    for side, target, count, start, border in (
        (0, left_ref, lefts, EDGE, EDGE + STEPS),
        (1, right_ref, rights, BX - STEPS, BX - STEPS - 1),
    ):

        @pl.when(count > 0)
        def _():
            for direction in range(DIRS):
                for half in range(HALVES):
                    target[0, direction, half, start : start + STEPS, :] = own_ref[
                        direction, half, side * STEPS : (side + 1) * STEPS, :
                    ]
            for step in range(STEPS):
                for at in range(5):
                    for half in range(HALVES):
                        target[step + 1, TOWARD[side][at], half, border, :] = cross_ref[
                            ((step * 2 + side) * 5 + at) * HALVES + half, :
                        ]

    tables = moves()
    skips = [jnp.where(here, 1, 0) for here in (outer_left, outer_right)]

    def groups_of(side, count):
        if count == 1:
            return [(EDGE - STEPS if side == 0 else BX - STEPS, 0, 8)]
        if side == 0:
            return [(PAD, 0, 8), (PAD + 8, 0, 8), (EDGE, 0, STEPS)]
        return [(PAD, STEPS, STEPS), (BX, 0, 8), (BX + 8, 0, 8)]

    strips = (left_ref, right_ref)

    def put(target, group, halves):
        row, low, count = group
        for half in range(HALVES):
            for direction in range(DIRS):
                value = halves[half][direction]
                target[direction, half, row + low : row + low + count, :] = value[low : low + count, :]

    def plain(side, count, start):
        groups, strip = groups_of(side, count), strips[side]

        def body(step, carry):
            cells = [fetch(strip.at[step], group[0], jnp.minimum(step, 1)) for group in groups]
            relaxed = [shift([collide(half) for half in halves], tables) for halves in cells]
            for group, halves in zip(groups, relaxed):
                put(strip.at[step + 1], group, halves)
            return carry

        lax.fori_loop(start, STEPS, body, 0)

    def staggered(first, first_count, second_count):
        one, two = strips[first], strips[1 - first]
        first_groups, second_groups = groups_of(first, first_count), groups_of(1 - first, second_count)

        def settle(into):
            for at, group in enumerate(second_groups):
                put(two.at[into], group, shift(fetch(raw_ref, 8 * at, 0), tables))

        def body(step, carry):
            moved = jnp.minimum(step, 1)
            settle(jnp.where(step <= skips[1 - first], STEPS + 1, step))
            into = jnp.where(step < skips[first], STEPS + 1, step + 1)
            cells = [fetch(one.at[step], group[0], moved) for group in first_groups]
            relaxed = [[collide(half) for half in halves] for halves in cells]
            for group, halves in zip(first_groups, relaxed):
                put(one.at[into], group, shift(halves, tables))
            cells = [fetch(two.at[step], group[0], moved) for group in second_groups]
            relaxed = [[collide(half) for half in halves] for halves in cells]
            for at, halves in enumerate(relaxed):
                store(raw_ref, 8 * at, halves)
            return carry

        lax.fori_loop(0, STEPS, body, 0)
        settle(STEPS)

    for first, counts in ((0, (1, 1)), (0, (3, 1)), (1, (1, 3)), (0, (3, 3))):

        @pl.when(both(lefts == counts[0], rights == counts[1]))
        def _():
            staggered(first, counts[first], counts[1 - first])

    for count in (1, 3):

        @pl.when(both(lefts == count, rights == 0))
        def _():
            plain(0, count, skips[0])

        @pl.when(both(lefts == 0, rights == count))
        def _():
            plain(1, count, skips[1])

    row = held_old - 8 - offset
    ends = (
        (lefts, 0, left_ref, (16, EDGE), [(0, PAD), (8, PAD + 8)], 0, left_done_ref),
        (rights, 1, right_ref, (0, PAD), [(8, BX), (16, BX + 8)], row, right_done_ref),
    )
    for count, side, source, merged, whole, to, done in ends:
        for amount, used in ((3, whole), (1, [])):

            @pl.when(count == amount)
            def _():
                finish(side, source.at[STEPS], merged, used, to, edge_ref, out_ref, done, sem.at[side])

    for count, side, _, merged, whole, to, done in ends:
        for amount in (3, 1):

            @pl.when(count == amount)
            def _():
                size = 8 * amount
                start = 0 if amount == 3 else merged[0]
                pltpu.make_async_copy(
                    done.at[:, start : start + size, :],
                    out_ref.at[:, pl.ds(pl.multiple_of(to, 8), size), :],
                    sem.at[side],
                ).wait()


def shards(populations, count_old, count_new):
    curve_count, sub_count = lax.axis_size("curve"), lax.axis_size("sub")
    planes = populations.shape[1]
    slots = planes // BX
    total = curve_count * sub_count
    old, new = count_old.T, count_new.T
    smem = pl.BlockSpec(memory_space=pltpu.SMEM)
    hbm = pl.BlockSpec(memory_space=pltpu.HBM)
    vmem = pl.BlockSpec(memory_space=pltpu.VMEM)
    rows = DIRS * HALVES
    whole = jax.ShapeDtypeStruct(populations.shape, jnp.float32)

    def local(*shape):
        return pltpu.VMEM(shape, jnp.float32)

    def near(value):
        return pltpu.with_memory_space_constraint(value, pltpu.VMEM)

    params = pltpu.CompilerParams(vmem_limit_bytes=32 << 20)
    populations, old, new = (
        pltpu.with_memory_space_constraint(value, pltpu.HBM) for value in (populations, old, new)
    )
    one, two, cells, info = pl.pallas_call(
        functools.partial(pack_kernel, sub_count),
        out_shape=(
            local(rows * SPLIT, LANES),
            local(rows * SPLIT_TWO, LANES),
            local(DIRS, HALVES, planes, LANES),
            pltpu.SMEM((4,), jnp.int32),
        ),
        in_specs=[hbm, hbm, hbm],
        out_specs=(vmem, vmem, vmem, smem),
        scratch_shapes=[
            pltpu.SMEM(old.shape, jnp.int32),
            pltpu.SMEM(old.shape, jnp.int32),
            pltpu.SemaphoreType.DMA((2 + HALVES,)),
        ],
        compiler_params=params,
        name="pack",
    )(old, new, populations)
    info = pltpu.with_memory_space_constraint(info, pltpu.SMEM)
    cells = near(cells)
    axes = ("curve", "sub")

    def everyone(pairs):
        busy = {source for source, _ in pairs}
        rest = [at for at in range(total) if at not in busy]
        return pairs + [(at, (at // sub_count ^ 1) * sub_count + at % sub_count) for at in rest]

    def send(value, pairs):
        return lax.ppermute(value, axes, pairs)

    inside = [(at, at ^ 1) for at in range(total)]
    between, across = [], []
    for at in range(1, total, 2):
        after = (at + 1) % total
        into = across if after % sub_count == 0 else between
        into += [(at, after), (after, at)]
    sooner = [(at, beside) for at, beside in inside if at % sub_count // 2 % 2 == 0]
    later = [(at, beside) for at, beside in inside if at % sub_count // 2 % 2 == 1]
    ends = one
    one = send(ends, everyone(sooner))
    two = send(two, everyone(between))
    also = send(ends, everyone(later))
    rim = pl.pallas_call(
        functools.partial(rim_kernel, sub_count),
        out_shape=local(RIM, LANES),
        in_specs=[smem, vmem],
        out_specs=vmem,
        compiler_params=params,
        name="rim",
    )(info, cells)
    around = pltpu.VMEM((2, DIRS, HALVES, 3 * PAD, LANES), jnp.float32)
    more, last = pl.pallas_call(
        functools.partial(ahead_kernel, sub_count, True),
        out_shape=(local(more_rows(SPLIT), LANES), local(more_rows(SPLIT_TWO), LANES)),
        in_specs=[smem, vmem],
        out_specs=(vmem, vmem),
        scratch_shapes=[around, around],
        compiler_params=params,
        cost_estimate=pl.CostEstimate(flops=10**6, bytes_accessed=10**5, transcendentals=0),
        name="ahead_first",
    )(info, cells)
    first_done = more
    rim = send(lax.optimization_barrier((rim, first_done))[0], everyone(across))
    more, last = pl.pallas_call(
        functools.partial(ahead_kernel, sub_count, False),
        out_shape=(local(more_rows(SPLIT), LANES), local(more_rows(SPLIT_TWO), LANES)),
        in_specs=[smem, vmem, vmem, vmem],
        out_specs=(vmem, vmem),
        scratch_shapes=[around, around],
        input_output_aliases={2: 0, 3: 1},
        compiler_params=params,
        cost_estimate=pl.CostEstimate(flops=10**6, bytes_accessed=10**5, transcendentals=0),
        name="ahead",
    )(info, cells, near(more), near(last))
    last = send(last, everyone(between))
    more = send(more, inside)
    state = pltpu.VMEM((DIRS, HALVES, planes + 2 * PAD, LANES), jnp.float32)
    result, own, following, cross, edge = pl.pallas_call(
        functools.partial(inner_kernel, slots),
        out_shape=(
            whole,
            local(DIRS, HALVES, 2 * STEPS, LANES),
            local(DIRS, HALVES, 2 * STEPS, LANES),
            local(STEPS * 2 * 5 * HALVES, LANES),
            local(DIRS, 16, HALVES * LANES),
        ),
        in_specs=[smem, vmem],
        out_specs=(hbm, vmem, vmem, vmem, vmem),
        scratch_shapes=[
            state,
            state,
            pltpu.VMEM((DIRS, HALVES, 16, LANES), jnp.float32),
            pltpu.VMEM(populations.shape, jnp.float32),
            pltpu.VMEM((DIRS, BX, HALVES * LANES), jnp.float32),
            pltpu.SemaphoreType.DMA((slots + slots * BX // 8,)),
        ],
        compiler_params=params,
        cost_estimate=pl.CostEstimate(flops=10**9, bytes_accessed=8 * 10**6, transcendentals=0),
        name="inner",
    )(info, cells)
    own, following, cross, edge = map(near, (own, following, cross, edge))
    return pl.pallas_call(
        functools.partial(tail_kernel, sub_count),
        out_shape=whole,
        in_specs=[smem] + [vmem] * 10 + [hbm],
        out_specs=hbm,
        scratch_shapes=[
            pltpu.VMEM((STEPS + 2, DIRS, HALVES, STRIP, LANES), jnp.float32),
            pltpu.VMEM((STEPS + 2, DIRS, HALVES, STRIP, LANES), jnp.float32),
            pltpu.VMEM((DIRS, HALVES, 24, LANES), jnp.float32),
            pltpu.VMEM((DIRS, 24, HALVES * LANES), jnp.float32),
            pltpu.VMEM((DIRS, 24, HALVES * LANES), jnp.float32),
            pltpu.SemaphoreType.DMA((2,)),
        ],
        input_output_aliases={11: 0},
        compiler_params=params,
        cost_estimate=pl.CostEstimate(flops=10**8, bytes_accessed=10**6, transcendentals=0),
        name="tail",
    )(info, own, following, cross, edge, *map(near, (one, also, more, two, last, rim)), result)


def solution(mesh):
    if mesh.shape["sub"] % 2 or mesh.shape["curve"] % 2:
        raise ValueError("odd mesh")
    in_specs = (P(None, ("curve", "sub"), None), P(), P())
    out_specs = P(None, ("curve", "sub"), None)
    return jax.shard_map(shards, mesh=mesh, in_specs=in_specs, out_specs=out_specs, check_vma=False)
```
